128 devices in a mesh: row: 4 (over y), col: 32 (over x, z, core).
Axes of the slice: x: 4, y: 4, z: 4, core: 2. Of those that a mesh axis runs over, the one named last changes fastest.
Arguments:
- coordinates: float32 [3, 65536], replicated, may hold values from 0 to 1
- ordering: int32 [65536], replicated, may hold values from 0 to 65535, each once
- neighbours: int32 [256, 4], replicated, may hold values from 0 to 254, as said below
- cross: float32 [256, 4, 256, 256], P(('row', 'col')), may hold values from -0.1875 to 0.1875
- whitening: float32 [256, 256, 256], P(('row', 'col')), may hold values from -0.1875 to 0.1875
- solution: float32 [256, 8, 256], P(('row', 'col')), may hold values from -6 to 6
- residual: float32 [256, 8, 256], P(('row', 'col')), may hold values from -40 to 40
- direction: float32 [256, 8, 256], P(('row', 'col')), may hold values from -40 to 40
Outputs:
- solution_next: float32 [256, 8, 256], P(('row', 'col'))
- residual_next: float32 [256, 8, 256], P(('row', 'col'))
- direction_next: float32 [256, 8, 256], P(('row', 'col'))
The draws below stay inside these ranges and needn't reach their ends.
Inputs may be any that keep to these rules, and one draw needn't show every extreme that they name: `neighbours`: row b lists b - 1 first, then further distinct blocks below b - 1; where fewer than 4 earlier blocks exist the remaining entries equal b itself.
All inputs are finite; a program needn't handle non-finite values.
Results may differ from the reference program's by a relative error of at most 0.00023.
Values sent between devices are 32-bit elements; how exact they have to be, the bound alone decides.
No kernel may reach another device: no remote copies, remote signals or barrier semaphores. Data moves between devices by JAX's collectives and lax.ppermute only.
A program may use at most 192 MiB of HBM per device.

```python
import math
import jax
import jax.numpy as jnp
from jax import lax

BS = 256
NBR = 4
RHS = 8
NBLK = 256
NPTS = 65536


def draw_neighbours(key, part):
    key = jax.random.fold_in(key, 5)
    blocks = jnp.arange(NBLK, dtype=jnp.int32)[:, None]
    others = jnp.arange(NBLK, dtype=jnp.int32)[None, :]
    scores = jax.random.randint(key, (NBLK, NBLK), 0, 2 ** 19, dtype=jnp.int32)
    ranked = jnp.where(others < blocks - 1, scores * 2048 + others, -1 - others)
    chosen = lax.top_k(ranked, NBR - 1)[1].astype(jnp.int32)
    chosen = jnp.where(chosen < blocks - 1, chosen, blocks)
    previous = jnp.maximum(blocks - 1, 0)
    return jnp.concatenate([previous, chosen], axis=1).astype(jnp.int32)


def draw_scaled(key):
    position = (jnp.arange(NBLK)[:, None, None] * BS + jnp.arange(BS)[None, None, :]).astype(jnp.float32) / NPTS
    column = jnp.arange(RHS).astype(jnp.float32)[None, :, None] / (RHS - 1)
    base = jax.random.truncated_normal(key, -4.0, 4.0, (NBLK, RHS, BS), jnp.float32)
    scales = 10.0 ** (position - 0.5)
    return (base * scales * 10.0 ** (column - 0.5)).astype(jnp.float32)


def draw_residual(key, part):
    return draw_scaled(jax.random.fold_in(key, 11))


def draw_direction(key, part):
    return draw_scaled(jax.random.fold_in(key, 23))


def levels(own_key, extent, split, low, largest):
    level, own = 1.0, jax.random.fold_in(own_key, 6)
    for axis_at, shards_of in split:
        heights = jnp.exp(jax.random.uniform(jax.random.fold_in(own, axis_at), (shards_of,), jnp.float32, low / len(split), largest / len(split)))
        level = level * jnp.repeat(heights, extent[axis_at] // shards_of).reshape([-1 if axis == axis_at else 1 for axis in range(len(extent))])
    return level


def centred(own_key, extent, deviation, reach, cuts=(), kind=jnp.bfloat16):
    loudness = levels(own_key, extent, cuts, -0.22, 0.18) if cuts else 1.0
    array = jax.random.normal(own_key, extent, jnp.float32) * deviation * loudness
    return jnp.minimum(jnp.maximum(array, -reach), reach).astype(kind)


def setup_inputs(seed: int = 0) -> dict:
    seeds = jax.random.split(jax.random.key(seed), 9)
    return {
        "coordinates": jnp.clip(jax.random.uniform(seeds[0], (3, NPTS), jnp.float32, 0.0, 1.0), 0.0, 1.0),
        "ordering": jax.random.permutation(seeds[1], NPTS).astype(jnp.int32),
        "neighbours": draw_neighbours(jax.random.fold_in(seeds[8], 71), 0),
        "cross": centred(seeds[3], (NBLK, NBR, BS, BS), (NBR * BS) ** -0.5, 0.1875, ((0, 128),), jnp.float32),
        "whitening": centred(seeds[4], (NBLK, BS, BS), (NBR * BS) ** -0.5, 0.1875, ((0, 128),), jnp.float32),
        "solution": centred(seeds[5], (NBLK, RHS, BS), 1.0, 6.0, ((0, 128),), jnp.float32),
        "residual": draw_residual(jax.random.fold_in(seeds[8], 71), 0),
        "direction": draw_direction(jax.random.fold_in(seeds[8], 71), 0),
    }


kernel_rate = math.sqrt(3.0) / 0.3
variance = 0.05
nugget = 1.0
highest = lax.Precision.HIGHEST

def covariance(rows, columns):
    apart_x = rows[0][:, None] - columns[0][None, :]
    apart_y = rows[1][:, None] - columns[1][None, :]
    apart_z = rows[2][:, None] - columns[2][None, :]
    distance = jnp.sqrt(apart_x * apart_x + apart_y * apart_y + apart_z * apart_z)
    scaled = kernel_rate * distance
    return variance * (1.0 + scaled) * jnp.exp(-scaled)

def precondition(field, neighbours, cross, whitening):
    count = field.shape[0]
    block_ids = jnp.arange(count, dtype=jnp.int32)
    valid = (neighbours < block_ids[:, None]).astype(jnp.float32)
    near = field[neighbours] * valid[:, :, None, None]
    lowered = field - jnp.einsum('bkcj,bkij->bci', near, cross, precision=highest)
    whiten = whitening + jnp.eye(BS, dtype=jnp.float32)[None]
    mapped = jnp.einsum('bcj,bij->bci', lowered, whiten, precision=highest)
    scaled = jnp.einsum('bci,bij->bcj', mapped, whiten, precision=highest)
    spread = jnp.einsum('bci,bkij->bkcj', scaled, cross, precision=highest) * valid[:, :, None, None]
    back = jax.ops.segment_sum(spread.reshape(count * NBR, RHS, BS), neighbours.reshape(-1), num_segments=count)
    return scaled - back

def apply_kernel(points, field):
    flat_points = points.reshape(3, -1)
    flat_field = field.transpose(1, 0, 2).reshape(RHS, -1)

    def one_block(block_points):
        tile = covariance(block_points, flat_points)
        return lax.dot_general(flat_field, tile, (((1,), (1,)), ((), ())), precision=highest)
    blocks = lax.map(one_block, points.transpose(1, 0, 2))
    return blocks + nugget * field

def reference(coordinates, ordering, neighbours, cross, whitening, solution, residual, direction):
    points = coordinates[:, ordering].reshape(3, NBLK, BS)
    image = apply_kernel(points, direction)
    pre = precondition(residual, neighbours, cross, whitening)
    old = lax.optimization_barrier(jnp.sum(residual * pre, axis=(0, 2)))
    curvature = lax.optimization_barrier(jnp.sum(direction * image, axis=(0, 2)))
    step_size = (old / curvature)[None, :, None]
    solution_next = solution + step_size * direction
    residual_next = residual - step_size * image
    pre_next = precondition(residual_next, neighbours, cross, whitening)
    newer = lax.optimization_barrier(jnp.sum(residual_next * pre_next, axis=(0, 2)))
    ratio = (newer / old)[None, :, None]
    direction_next = pre_next + ratio * direction
    return (solution_next, residual_next, direction_next)
```

```python
import functools
import math

import jax
import jax.numpy as jnp
from jax import lax
from jax.experimental import pallas as pl
from jax.experimental.pallas import tpu as pltpu
from jax.sharding import PartitionSpec as P

f32 = jnp.float32
bf16 = jnp.bfloat16
highest = lax.Precision.HIGHEST
rate = math.sqrt(3.0) / 0.3 * math.log2(math.e)
offset = 1.0 / math.log(2.0)
variance = 0.05 * math.log(2.0)
nugget = 1.0
AXES = ("row", "col")
BS, RHS, NBR, OWN = 256, 8, 4, 2
HALF = 128
STEP = 4
MEGA = 1 << 20


def dot(a, b, dims):
    return lax.dot_general(a, b, (dims, ((), ())), precision=highest, preferred_element_type=f32)


def split2(v):
    top = v.astype(bf16)
    return top, (v - top.astype(f32)).astype(bf16)


def split3(v):
    top = v.astype(bf16).astype(f32)
    rest = v - top
    middle = rest.astype(bf16).astype(f32)
    return top, middle, rest - middle


def features(place, own):
    a = (place - 0.5) * rate
    norm = jnp.sum(a * a, axis=0, keepdims=True)
    one = jnp.ones_like(norm)
    pad = jnp.zeros((3, norm.shape[1]), f32)
    parts = [-2.0 * a, one, norm, pad] if own else [a, norm, one, pad]
    top, middle, low = split3(jnp.concatenate(parts, axis=0))
    order = [top, middle, top, middle, low, top] if own else [top, top, middle, middle, top, low]
    return jnp.concatenate(order, axis=0).astype(bf16)


def places(tiles, block):
    rows = slice(3 * block, 3 * block + 3)
    return jnp.concatenate([tiles[4, rows, :], tiles[5, rows, :]], axis=1)


def pick_points(order_ref, coordinates_ref, direction_ref, out_ref):
    lane = lax.broadcasted_iota(jnp.int32, (3, HALF), 1)
    for block in range(OWN):
        for half in range(2):
            out_ref[2 * block + half] = direction_ref[block, :, half * HALF : (half + 1) * HALF]
    out_ref[4] = jnp.zeros((RHS, HALF), f32)
    out_ref[5] = jnp.zeros((RHS, HALF), f32)
    for group in range(2 * OWN):

        def one_point(i, found, group=group):
            at = order_ref[group * HALF + i]
            base = pl.multiple_of((at >> 7) << 7, HALF)
            line = coordinates_ref[:, pl.ds(base, HALF)]
            turned = pltpu.roll(line, (i - (at & (HALF - 1))) & (HALF - 1), 1)
            return jnp.where(lane == i, turned, found)

        found = lax.fori_loop(0, HALF, one_point, jnp.zeros((3, HALF), f32), unroll=8)
        block, half = group // 2, group % 2
        out_ref[4 + half, 3 * block : 3 * block + 3, :] = found


def point_payload(own_order, coordinates, direction):
    return pl.pallas_call(
        pick_points,
        out_shape=jax.ShapeDtypeStruct((6, RHS, HALF), f32),
        in_specs=[
            pl.BlockSpec(memory_space=pltpu.SMEM),
            pl.BlockSpec(memory_space=pltpu.VMEM),
            pl.BlockSpec(memory_space=pltpu.VMEM),
        ],
        out_specs=pl.BlockSpec(memory_space=pltpu.VMEM),
        compiler_params=pltpu.CompilerParams(vmem_limit_bytes=8 * MEGA),
        name="pick_points",
    )(own_order, coordinates, direction)


TALL, WIDE = 512, 256


def image_kernel(own_ref, columns_ref, start_ref, out_ref, own_part, column_part, field_part, square):
    @pl.when(pl.program_id(0) == 0)
    def _():
        for block in range(OWN):
            own_part[:, block * BS : (block + 1) * BS] = features(places(own_ref, block), True)
        out_ref[...] = start_ref[...]

    for member in range(STEP):
        for block in range(OWN):
            at = OWN * member + block
            tiles = columns_ref.at[member]
            column_part[at * BS : (at + 1) * BS, :] = features(places(tiles, block), False).T
            field = jnp.concatenate([tiles[2 * block], tiles[2 * block + 1]], axis=1) * variance
            field_part[at] = jnp.concatenate(split2(field), axis=0)
    jobs = [
        (q, r) for r in range(OWN * BS // WIDE) for q in range(STEP * OWN * BS // TALL)
    ]

    def fill(job, slot):
        q, r = jobs[job]
        square[slot] = jnp.dot(
            column_part[q * TALL : (q + 1) * TALL, :],
            own_part[:, r * WIDE : (r + 1) * WIDE],
            preferred_element_type=f32,
        )

    fill(0, 0)
    for job, (q, r) in enumerate(jobs):
        if job + 1 < len(jobs):
            fill(job + 1, (job + 1) % 2)
        for part in range(TALL // BS):
            for lanes in range(WIDE // HALF):
                x = square[
                    job % 2, part * BS : (part + 1) * BS, lanes * HALF : (lanes + 1) * HALF
                ]
                x = jnp.maximum(x, 1e-30)
                t = x * lax.rsqrt(x)
                tile = (t + offset) * jnp.exp2(-t)
                top, low = split2(tile)
                field = field_part[q * (TALL // BS) + part]
                where = slice(r * WIDE + lanes * HALF, r * WIDE + (lanes + 1) * HALF)
                out_ref[:, where] += jnp.dot(
                    field, top, preferred_element_type=f32
                ) + jnp.dot(field, low, preferred_element_type=f32)


def add_image(own, columns, start):
    count = columns.shape[0]
    pairs = count * OWN * BS * OWN * BS
    return pl.pallas_call(
        image_kernel,
        grid=(count // STEP,),
        in_specs=[
            pl.BlockSpec((6, RHS, HALF), lambda i: (0, 0, 0)),
            pl.BlockSpec((STEP, 6, RHS, HALF), lambda i: (i, 0, 0, 0)),
            pl.BlockSpec((2 * RHS, OWN * BS), lambda i: (0, 0)),
        ],
        out_specs=pl.BlockSpec((2 * RHS, OWN * BS), lambda i: (0, 0)),
        out_shape=jax.ShapeDtypeStruct((2 * RHS, OWN * BS), f32),
        scratch_shapes=[
            pltpu.VMEM((48, OWN * BS), bf16),
            pltpu.VMEM((STEP * OWN * BS, 48), bf16),
            pltpu.VMEM((OWN * STEP, 2 * RHS, BS), bf16),
            pltpu.VMEM((2, TALL, WIDE), f32),
        ],
        compiler_params=pltpu.CompilerParams(vmem_limit_bytes=24 * MEGA),
        cost_estimate=pl.CostEstimate(
            flops=1200 * pairs, transcendentals=2 * pairs, bytes_accessed=count * 6 * 4096
        ),
        name="image",
    )(own, columns, start)


def lower(near, valid_ref, cross_ref, field, block):
    total = field
    for k in range(NBR):
        weight = valid_ref[block * NBR + k].astype(f32)
        total = total - dot(near(block, k) * weight, cross_ref[block, k], ((1,), (1,)))
    return total


def whiten_of(whitening_ref, block):
    rows = lax.broadcasted_iota(jnp.int32, (BS, BS), 0)
    lanes = lax.broadcasted_iota(jnp.int32, (BS, BS), 1)
    return whitening_ref[block] + jnp.where(rows == lanes, 1.0, 0.0)


def lanes_of(v):
    return v[:, :HALF] + v[:, HALF:]


def measure_kernel(
    list_ref, valid_ref, all_ref, residual_ref, cross_ref, whitening_ref, sum_ref, direction_ref,
    out_ref, near_ref, near_buf, sems,
):
    copies = []
    for b in range(OWN):
        for k in range(NBR):
            at = b * NBR + k
            copies.append(
                pltpu.make_async_copy(all_ref.at[list_ref[at]], near_buf.at[at], sems.at[at])
            )
            copies[-1].start()
    for copy in copies:
        copy.wait()
    old = jnp.zeros((RHS, HALF), f32)
    curvature = jnp.zeros((RHS, HALF), f32)
    for b in range(OWN):
        lowered = lower(
            lambda b, k: near_buf[b * NBR + k], valid_ref, cross_ref, residual_ref[b], b
        )
        mapped = dot(lowered, whiten_of(whitening_ref, b), ((1,), (1,)))
        old = old + lanes_of(mapped * mapped)
        here = slice(b * BS, (b + 1) * BS)
        image = sum_ref[:RHS, here] + sum_ref[RHS:, here] + nugget * direction_ref[b]
        curvature = curvature + lanes_of(direction_ref[b] * image)
        out_ref[2 * b] = image[:, :HALF]
        out_ref[2 * b + 1] = image[:, HALF:]
    lane = lax.broadcasted_iota(jnp.int32, (RHS, HALF), 1)
    old = jnp.sum(old, axis=1, keepdims=True)
    curvature = jnp.sum(curvature, axis=1, keepdims=True)
    out_ref[4] = jnp.where(lane == 0, old, jnp.where(lane == 1, curvature, 0.0))
    near_ref[...] = near_buf[...]


def measure_step(lists, valid, gathered, residual, cross, whitening, total, direction):
    smem = pl.BlockSpec(memory_space=pltpu.SMEM)
    vmem = pl.BlockSpec(memory_space=pltpu.VMEM)
    return pl.pallas_call(
        measure_kernel,
        out_shape=(
            jax.ShapeDtypeStruct((5, RHS, HALF), f32),
            jax.ShapeDtypeStruct((OWN * NBR, RHS, BS), f32),
        ),
        in_specs=[smem, smem, pl.BlockSpec(memory_space=pl.ANY), vmem, vmem, vmem, vmem, vmem],
        out_specs=(vmem, vmem),
        scratch_shapes=[
            pltpu.VMEM((OWN * NBR, RHS, BS), f32),
            pltpu.SemaphoreType.DMA((OWN * NBR,)),
        ],
        compiler_params=pltpu.CompilerParams(vmem_limit_bytes=24 * MEGA),
        name="measure_step",
    )(lists, valid, gathered, residual, cross, whitening, total, direction)


def spread_kernel(
    at_ref, valid_ref, into_ref, mine_ref, other_ref, near_ref, residual_ref, solution_ref,
    direction_ref, cross_ref, whitening_ref,
    solution_out, residual_out, scaled_out, out_ref, scalar_out,
):
    total = jnp.zeros((RHS, HALF), f32)
    for i in range(64):
        total = total + mine_ref[i, 4] + other_ref[i, 4]
    old = total[:, 0:1]
    step = old / total[:, 1:2]

    out_ref[...] = jnp.zeros_like(out_ref)

    def image_of(at):
        slot = at & 63
        a = jnp.concatenate([mine_ref[slot, 2 * (at >> 7)], mine_ref[slot, 2 * (at >> 7) + 1]], 1)
        b = jnp.concatenate([other_ref[slot, 2 * (at >> 7)], other_ref[slot, 2 * (at >> 7) + 1]], 1)
        return jnp.where(((at >> 6) & 1) == 0, a, b)

    newer = jnp.zeros((RHS, HALF), f32)
    for b in range(OWN):
        solution_out[b] = solution_ref[b] + step * direction_ref[b]
        image = jnp.concatenate([mine_ref[0, 2 * b], mine_ref[0, 2 * b + 1]], 1)
        following = residual_ref[b] - step * image
        residual_out[b] = following
        lowered = lower(
            lambda b, k: near_ref[b * NBR + k] - step * image_of(at_ref[b * NBR + k]),
            valid_ref, cross_ref, following, b,
        )
        whiten = whiten_of(whitening_ref, b)
        mapped = dot(lowered, whiten, ((1,), (1,)))
        newer = newer + lanes_of(mapped * mapped)
        scaled = dot(mapped, whiten, ((1,), (0,)))
        scaled_out[b] = scaled
        for k in range(NBR):
            at = b * NBR + k
            spread = dot(scaled, cross_ref[b, k], ((1,), (0,))) * valid_ref[at].astype(f32)
            to = into_ref[at]
            out_ref[pl.ds(2 * to, 1)] += spread[None, :, :HALF]
            out_ref[pl.ds(2 * to + 1, 1)] += spread[None, :, HALF:]
    newer = jnp.sum(newer, axis=1, keepdims=True)
    lane = lax.broadcasted_iota(jnp.int32, (RHS, HALF), 1)
    scalar_out[0] = jnp.where(lane == 0, newer, 0.0)
    scalar_out[1] = jnp.where(lane == 0, old, 0.0)


def spread_step(at, valid, into, mine, other, near, residual, solution, direction, cross, whitening):
    smem = pl.BlockSpec(memory_space=pltpu.SMEM)
    vmem = pl.BlockSpec(memory_space=pltpu.VMEM)
    own = jax.ShapeDtypeStruct((OWN, RHS, BS), f32)
    return pl.pallas_call(
        spread_kernel,
        out_shape=(
            own,
            own,
            own,
            jax.ShapeDtypeStruct((128 * 2 * OWN, RHS, HALF), f32),
            jax.ShapeDtypeStruct((2, RHS, HALF), f32),
        ),
        in_specs=[smem] * 3 + [vmem] * 8,
        out_specs=(vmem,) * 5,
        compiler_params=pltpu.CompilerParams(vmem_limit_bytes=40 * MEGA),
        name="spread_step",
    )(at, valid, into, mine, other, near, residual, solution, direction, cross, whitening)


def around(axis, hop):
    def target(i):
        x, z, core = i // 8, (i // 2) % 4, i % 2
        if axis == "x":
            x = (x + hop) % 4
        elif axis == "z":
            z = (z + hop) % 4
        else:
            core = core ^ hop
        return (x * 4 + z) * 2 + core

    if axis == "y":
        return functools.partial(
            lax.ppermute, axis_name="row", perm=[(i, (i + hop) % 4) for i in range(4)]
        )
    return functools.partial(
        lax.ppermute, axis_name="col", perm=[(i, target(i)) for i in range(32)]
    )


def gather_along(axis, value):
    return jnp.stack([value] + [around(axis, hop)(value) for hop in (1, 2, 3)])


def per_device(coordinates, ordering, neighbours, cross, whitening, solution, residual, direction):
    row = lax.axis_index("row")
    col = lax.axis_index("col")
    device = row * 32 + col
    here_x, here_z, here_core = col // 8, (col // 2) % 4, col % 2
    own_ids = device * OWN + jnp.arange(OWN, dtype=jnp.int32)
    own_lists = lax.dynamic_slice_in_dim(neighbours, device * OWN, OWN, 0)
    valid = (own_lists < own_ids[:, None]).astype(jnp.int32).reshape(-1)
    lists = own_lists.reshape(-1)
    their = lists // OWN
    their_y, their_x, their_z, their_core = their // 32, (their // 8) % 4, (their // 2) % 4, their % 2
    core_gap = their_core ^ here_core
    at = (
        ((lists % OWN) * 2 + core_gap) * 64
        + ((here_x - their_x) % 4) * 16
        + ((here_z - their_z) % 4) * 4
        + (row - their_y) % 4
    )
    into = (
        ((core_gap * 4 + (their_x - here_x) % 4) * 4 + (their_z - here_z) % 4) * 4
        + (their_y - row) % 4
    ) * OWN + lists % OWN

    gathered = lax.all_gather(residual, AXES, axis=0, tiled=True)

    own_order = lax.dynamic_slice_in_dim(ordering, device * (OWN * BS), OWN * BS, 0)
    own = point_payload(own_order, coordinates, direction)
    line = gather_along("y", own)
    plane = gather_along("z", line).reshape(16, 6, RHS, HALF)
    beyond = [around("x", hop)(plane) for hop in (1, 2, 3)]
    plane_other = around("core", 1)(plane)
    start = jnp.zeros((2 * RHS, OWN * BS), f32)
    total = add_image(own, plane, start)
    total = add_image(own, plane_other, total)
    for piece in beyond:
        total = add_image(own, piece, total)
    others = [around("core", 1)(piece) for piece in beyond]
    for piece in others:
        total = add_image(own, piece, total)

    image, near = measure_step(
        lists, valid, gathered, residual, cross, whitening, total, direction
    )
    line = gather_along("y", image)
    plane = gather_along("z", line)
    mine = gather_along("x", plane).reshape(64, 5, RHS, HALF)
    other = around("core", 1)(mine)
    solution_next, residual_next, scaled, back, scalars = spread_step(
        at, valid, into, mine, other, near, residual, solution, direction, cross, whitening
    )
    back = back.reshape(2, 4, 4, 4, 2 * OWN, RHS, HALF)
    back = back[0] + around("core", 1)(back[1])
    old, scalars = scalars[1, :, 0], scalars[:1]
    scalars = scalars + around("core", 1)(scalars)
    for axis in ("x", "z", "y"):
        back = back[0] + sum(around(axis, hop)(back[hop]) for hop in (1, 2, 3))
        scalars = scalars + sum(around(axis, hop)(scalars) for hop in (1, 2, 3))
    back = back.reshape(OWN, 2, RHS, HALF).transpose(0, 2, 1, 3).reshape(OWN, RHS, BS)
    newer = scalars[0, :, 0]
    ratio = (newer / old)[None, :, None]
    direction_next = scaled - back + ratio * direction
    return (solution_next, residual_next, direction_next)


def solution(mesh):
    placed = (
        P(),
        P(),
        P(),
        P(("row", "col"), None, None, None),
        P(("row", "col"), None, None),
        P(("row", "col"), None, None),
        P(("row", "col"), None, None),
        P(("row", "col"), None, None),
    )
    return jax.shard_map(
        per_device,
        mesh=mesh,
        in_specs=placed,
        out_specs=(
            P(("row", "col"), None, None),
            P(("row", "col"), None, None),
            P(("row", "col"), None, None),
        ),
        check_vma=False,
    )
```

```python
import functools
import math

import jax
import jax.numpy as jnp
from jax import lax
from jax.experimental import pallas as pl
from jax.experimental.pallas import tpu as pltpu
from jax.sharding import PartitionSpec as P

f32 = jnp.float32
bf16 = jnp.bfloat16
highest = lax.Precision.HIGHEST
rate = math.sqrt(3.0) / 0.3 * math.log2(math.e)
offset = 1.0 / math.log(2.0)
variance = 0.05 * math.log(2.0)
nugget = 1.0
AXES = ("row", "col")
BS, RHS, NBR, OWN = 256, 8, 4, 2
HALF = 128
STEP = 4
PEERS = 64
MEGA = 1 << 20


def dot(a, b, dims):
    return lax.dot_general(a, b, (dims, ((), ())), precision=highest, preferred_element_type=f32)


def split2(v):
    top = v.astype(bf16)
    return top, (v - top.astype(f32)).astype(bf16)


def split3(v):
    top = v.astype(bf16).astype(f32)
    rest = v - top
    middle = rest.astype(bf16).astype(f32)
    return top, middle, rest - middle


def features(place, own):
    a = (place - 0.5) * rate
    norm = jnp.sum(a * a, axis=0, keepdims=True)
    one = jnp.ones_like(norm)
    pad = jnp.zeros((3, norm.shape[1]), f32)
    parts = [-2.0 * a, one, norm, pad] if own else [a, norm, one, pad]
    top, middle, low = split3(jnp.concatenate(parts, axis=0))
    order = [top, middle, top, middle, low, top] if own else [top, top, middle, middle, top, low]
    return jnp.concatenate(order, axis=0).astype(bf16)


def places(tiles, block):
    rows = slice(3 * block, 3 * block + 3)
    return jnp.concatenate([tiles[4, rows, :], tiles[5, rows, :]], axis=1)


def pick_points(order_ref, coordinates_ref, direction_ref, out_ref):
    lane = lax.broadcasted_iota(jnp.int32, (3, HALF), 1)
    groups = 2 * OWN

    def one_point(i, found):
        kept = []
        for group in range(groups):
            at = order_ref[group * HALF + i]
            base = pl.multiple_of((at >> 7) << 7, HALF)
            line = coordinates_ref[:, pl.ds(base, HALF)]
            turned = pltpu.roll(line, (i - (at & (HALF - 1))) & (HALF - 1), 1)
            kept.append(jnp.where(lane == i, turned, found[group]))
        return tuple(kept)

    found = lax.fori_loop(0, HALF, one_point, (jnp.zeros((3, HALF), f32),) * groups, unroll=4)
    pad = jnp.zeros((2, HALF), f32)
    tiles = []
    for block in range(OWN):
        for half in range(2):
            tiles.append(direction_ref[block, :, half * HALF : (half + 1) * HALF])
    for half in range(2):
        tiles.append(jnp.concatenate([found[half], found[2 + half], pad], axis=0))

    def copy(i, carry):
        for part, tile in enumerate(tiles):
            out_ref[i, part] = tile
        return carry

    lax.fori_loop(0, out_ref.shape[0], copy, 0)


def point_payload(own_order, coordinates, direction, copies):
    return pl.pallas_call(
        pick_points,
        out_shape=jax.ShapeDtypeStruct((copies, 6, RHS, HALF), f32),
        in_specs=[
            pl.BlockSpec(memory_space=pltpu.SMEM),
            pl.BlockSpec(memory_space=pltpu.VMEM),
            pl.BlockSpec(memory_space=pltpu.VMEM),
        ],
        out_specs=pl.BlockSpec(memory_space=pltpu.VMEM),
        compiler_params=pltpu.CompilerParams(vmem_limit_bytes=8 * MEGA),
        name="pick_points",
    )(own_order, coordinates, direction)


TALL, WIDE = 512, 256


def image_kernel(pieces, own_ref, start_ref, *refs):
    columns, (out_ref, own_part, column_part, field_part, square) = refs[:pieces], refs[pieces:]
    each = pl.num_programs(0) // pieces

    @pl.when(pl.program_id(0) == 0)
    def _():
        for block in range(OWN):
            own_part[:, block * BS : (block + 1) * BS] = features(places(own_ref, block), True)
        out_ref[...] = start_ref[...]

    def prepare(columns_ref):
        for member in range(STEP):
            for block in range(OWN):
                at = OWN * member + block
                tiles = columns_ref.at[member]
                column_part[at * BS : (at + 1) * BS, :] = features(places(tiles, block), False).T
                field = jnp.concatenate([tiles[2 * block], tiles[2 * block + 1]], axis=1)
                field_part[at] = jnp.concatenate(split2(field * variance), axis=0)

    for index, columns_ref in enumerate(columns):
        pl.when(pl.program_id(0) // each == index)(functools.partial(prepare, columns_ref))
    jobs = [
        (q, r) for r in range(OWN * BS // WIDE) for q in range(STEP * OWN * BS // TALL)
    ]

    def fill(job, slot):
        q, r = jobs[job]
        square[slot] = jnp.dot(
            column_part[q * TALL : (q + 1) * TALL, :],
            own_part[:, r * WIDE : (r + 1) * WIDE],
            preferred_element_type=f32,
        )

    fill(0, 0)
    for job, (q, r) in enumerate(jobs):
        if job + 1 < len(jobs):
            fill(job + 1, (job + 1) % 2)
        for part in range(TALL // BS):
            for lanes in range(WIDE // HALF):
                x = square[
                    job % 2, part * BS : (part + 1) * BS, lanes * HALF : (lanes + 1) * HALF
                ]
                x = jnp.maximum(x, 1e-30)
                t = x * lax.rsqrt(x)
                tile = (t + offset) * jnp.exp2(-t)
                top, low = split2(tile)
                field = field_part[q * (TALL // BS) + part]
                where = slice(r * WIDE + lanes * HALF, r * WIDE + (lanes + 1) * HALF)
                out_ref[:, where] += jnp.dot(
                    field, top, preferred_element_type=f32
                ) + jnp.dot(field, low, preferred_element_type=f32)


def add_image(own, columns, start):
    pieces, count = len(columns), columns[0].shape[0]
    each = count // STEP
    pairs = pieces * count * OWN * BS * OWN * BS

    def piece_spec(index):
        return pl.BlockSpec(
            (STEP, 6, RHS, HALF),
            lambda i: (jnp.clip(i - index * each, 0, each - 1), 0, 0, 0),
        )

    return pl.pallas_call(
        functools.partial(image_kernel, pieces),
        grid=(pieces * each,),
        in_specs=[
            pl.BlockSpec((6, RHS, HALF), lambda i: (0, 0, 0)),
            pl.BlockSpec((2 * RHS, OWN * BS), lambda i: (0, 0)),
        ]
        + [piece_spec(index) for index in range(pieces)],
        out_specs=pl.BlockSpec((2 * RHS, OWN * BS), lambda i: (0, 0)),
        out_shape=jax.ShapeDtypeStruct((2 * RHS, OWN * BS), f32),
        scratch_shapes=[
            pltpu.VMEM((48, OWN * BS), bf16),
            pltpu.VMEM((STEP * OWN * BS, 48), bf16),
            pltpu.VMEM((OWN * STEP, 2 * RHS, BS), bf16),
            pltpu.VMEM((2, TALL, WIDE), f32),
        ],
        compiler_params=pltpu.CompilerParams(vmem_limit_bytes=24 * MEGA),
        cost_estimate=pl.CostEstimate(
            flops=600 * pairs, transcendentals=2 * pairs, bytes_accessed=pieces * count * 6 * 4096
        ),
        name="image",
    )(own, start, *columns)


def lower(near, valid_ref, cross_ref, field, block):
    total = field
    for k in range(NBR):
        weight = valid_ref[block * NBR + k].astype(f32)
        total = total - dot(near(block, k) * weight, cross_ref[block, k], ((1,), (1,)))
    return total


def whiten_of(whitening_ref, block):
    rows = lax.broadcasted_iota(jnp.int32, (BS, BS), 0)
    lanes = lax.broadcasted_iota(jnp.int32, (BS, BS), 1)
    return whitening_ref[block] + jnp.where(rows == lanes, 1.0, 0.0)


def lanes_of(v):
    return v[:, :HALF] + v[:, HALF:]


def measure_kernel(
    list_ref, valid_ref, all_ref, residual_ref, cross_ref, whitening_ref, sum_ref, direction_ref,
    out_ref, near_ref, near_buf, sems,
):
    copies = []
    for b in range(OWN):
        for k in range(NBR):
            at = b * NBR + k
            copies.append(
                pltpu.make_async_copy(all_ref.at[list_ref[at]], near_buf.at[at], sems.at[at])
            )
            copies[-1].start()
    for copy in copies:
        copy.wait()
    old = jnp.zeros((RHS, HALF), f32)
    curvature = jnp.zeros((RHS, HALF), f32)
    tiles = []
    for b in range(OWN):
        lowered = lower(
            lambda b, k: near_buf[b * NBR + k], valid_ref, cross_ref, residual_ref[b], b
        )
        mapped = dot(lowered, whiten_of(whitening_ref, b), ((1,), (1,)))
        old = old + lanes_of(mapped * mapped)
        here = slice(b * BS, (b + 1) * BS)
        image = sum_ref[:RHS, here] + sum_ref[RHS:, here] + nugget * direction_ref[b]
        curvature = curvature + lanes_of(direction_ref[b] * image)
        tiles += [image[:, :HALF], image[:, HALF:]]
    lane = lax.broadcasted_iota(jnp.int32, (RHS, HALF), 1)
    old = jnp.sum(old, axis=1, keepdims=True)
    curvature = jnp.sum(curvature, axis=1, keepdims=True)
    tiles.append(jnp.where(lane == 0, old, jnp.where(lane == 1, curvature, 0.0)))

    def copy(i, carry):
        for part, tile in enumerate(tiles):
            out_ref[i, part] = tile
        return carry

    lax.fori_loop(0, out_ref.shape[0], copy, 0)
    near_ref[...] = near_buf[...]


def measure_step(lists, valid, gathered, residual, cross, whitening, total, direction):
    smem = pl.BlockSpec(memory_space=pltpu.SMEM)
    vmem = pl.BlockSpec(memory_space=pltpu.VMEM)
    return pl.pallas_call(
        measure_kernel,
        out_shape=(
            jax.ShapeDtypeStruct((PEERS, 5, RHS, HALF), f32),
            jax.ShapeDtypeStruct((OWN * NBR, RHS, BS), f32),
        ),
        in_specs=[smem, smem, pl.BlockSpec(memory_space=pl.ANY), vmem, vmem, vmem, vmem, vmem],
        out_specs=(vmem, vmem),
        scratch_shapes=[
            pltpu.VMEM((OWN * NBR, RHS, BS), f32),
            pltpu.SemaphoreType.DMA((OWN * NBR,)),
        ],
        compiler_params=pltpu.CompilerParams(vmem_limit_bytes=24 * MEGA),
        name="measure_step",
    )(lists, valid, gathered, residual, cross, whitening, total, direction)


def spread_kernel(
    at_ref, valid_ref, into_ref, self_ref, mine_ref, other_ref, near_ref, residual_ref, solution_ref,
    direction_ref, cross_ref, whitening_ref,
    solution_out, residual_out, scaled_out, out_ref, old_out,
):
    total = jnp.zeros((RHS, HALF), f32)
    for i in range(PEERS):
        total = total + mine_ref[i, 4] + other_ref[i, 4]
    old = total[:, 0:1]
    step = old / total[:, 1:2]

    def clear(i, carry):
        for part in range(2 * OWN):
            out_ref[i, part] = jnp.zeros((RHS, HALF), f32)
        return carry

    lax.fori_loop(0, 2 * PEERS, clear, 0)

    def image_of(at):
        slot = at & 63
        a = jnp.concatenate([mine_ref[slot, 2 * (at >> 7)], mine_ref[slot, 2 * (at >> 7) + 1]], 1)
        b = jnp.concatenate([other_ref[slot, 2 * (at >> 7)], other_ref[slot, 2 * (at >> 7) + 1]], 1)
        return jnp.where(((at >> 6) & 1) == 0, a, b)

    newer = jnp.zeros((RHS, HALF), f32)
    for b in range(OWN):
        solution_out[b] = solution_ref[b] + step * direction_ref[b]
        image = jnp.concatenate(
            [mine_ref[self_ref[0], 2 * b], mine_ref[self_ref[0], 2 * b + 1]], 1
        )
        following = residual_ref[b] - step * image
        residual_out[b] = following
        lowered = lower(
            lambda b, k: near_ref[b * NBR + k] - step * image_of(at_ref[b * NBR + k]),
            valid_ref, cross_ref, following, b,
        )
        whiten = whiten_of(whitening_ref, b)
        mapped = dot(lowered, whiten, ((1,), (1,)))
        newer = newer + lanes_of(mapped * mapped)
        scaled = dot(mapped, whiten, ((1,), (0,)))
        scaled_out[b] = scaled
        for k in range(NBR):
            at = b * NBR + k
            spread = dot(scaled, cross_ref[b, k], ((1,), (0,))) * valid_ref[at].astype(f32)
            to = into_ref[at]
            out_ref[to >> 1, 2 * (to & 1)] += spread[:, :HALF]
            out_ref[to >> 1, 2 * (to & 1) + 1] += spread[:, HALF:]
    newer = jnp.sum(newer, axis=1, keepdims=True)
    lane = lax.broadcasted_iota(jnp.int32, (RHS, HALF), 1)
    newer = jnp.where(lane == 0, newer, 0.0)

    def share(i, carry):
        out_ref[i, 2 * OWN] = newer
        return carry

    lax.fori_loop(0, 2 * PEERS, share, 0)
    old_out[...] = jnp.broadcast_to(old, (RHS, HALF))


def sum_kernel(all_ref, scaled_ref, direction_ref, old_ref, out_ref):
    total = all_ref[0]
    for i in range(1, PEERS):
        total = total + all_ref[i]
    ratio = total[2 * OWN, :, 0:1] / old_ref[:, 0:1]
    for b in range(OWN):
        back = jnp.concatenate([total[2 * b], total[2 * b + 1]], axis=1)
        out_ref[b] = scaled_ref[b] - back + ratio * direction_ref[b]


def sum_step(everything, scaled, direction, old):
    vmem = pl.BlockSpec(memory_space=pltpu.VMEM)
    return pl.pallas_call(
        sum_kernel,
        out_shape=jax.ShapeDtypeStruct((OWN, RHS, BS), f32),
        in_specs=[vmem] * 4,
        out_specs=vmem,
        compiler_params=pltpu.CompilerParams(vmem_limit_bytes=8 * MEGA),
        name="sum_step",
    )(everything, scaled, direction, old)


def spread_step(
    at, valid, into, self_at, mine, other, near, residual, solution, direction, cross, whitening
):
    smem = pl.BlockSpec(memory_space=pltpu.SMEM)
    vmem = pl.BlockSpec(memory_space=pltpu.VMEM)
    own = jax.ShapeDtypeStruct((OWN, RHS, BS), f32)
    return pl.pallas_call(
        spread_kernel,
        out_shape=(
            own,
            own,
            own,
            jax.ShapeDtypeStruct((2 * PEERS, 2 * OWN + 1, RHS, HALF), f32),
            jax.ShapeDtypeStruct((RHS, HALF), f32),
        ),
        in_specs=[smem] * 4 + [vmem] * 8,
        out_specs=(vmem,) * 5,
        compiler_params=pltpu.CompilerParams(vmem_limit_bytes=40 * MEGA),
        name="spread_step",
    )(
        at, valid, into, self_at, mine, other, near, residual, solution, direction, cross,
        whitening,
    )


def x_around(hop):
    def target(i):
        return (i // 8 + hop) % 4 * 8 + i % 8

    return functools.partial(
        lax.ppermute, axis_name="col", perm=[(i, target(i)) for i in range(32)]
    )


def to_other_core(value):
    return lax.ppermute(value, "col", [(i, i ^ 1) for i in range(32)])


def exchange(value, groups):
    return lax.all_to_all(value, AXES, 0, 0, axis_index_groups=groups, tiled=True)


SAME_CORE = [[2 * j + core for j in range(PEERS)] for core in range(2)]
SAME_X = [
    [y * 32 + x * 8 + z * 2 + core for core in range(2) for y in range(4) for z in range(4)]
    for x in range(4)
]


def per_device(coordinates, ordering, neighbours, cross, whitening, solution, residual, direction):
    row = lax.axis_index("row")
    col = lax.axis_index("col")
    device = row * 32 + col
    here_core = device % 2
    own_ids = device * OWN + jnp.arange(OWN, dtype=jnp.int32)
    own_lists = lax.dynamic_slice_in_dim(neighbours, device * OWN, OWN, 0)
    valid = (own_lists < own_ids[:, None]).astype(jnp.int32).reshape(-1)
    lists = own_lists.reshape(-1)
    their = lists // OWN
    core_gap = (their % 2) ^ here_core
    at = ((lists % OWN) * 2 + core_gap) * PEERS + their // 2
    into = (core_gap * PEERS + their // 2) * OWN + lists % OWN
    self_at = (device // 2)[None]

    gathered = lax.all_gather(residual, AXES, axis=0, tiled=True)

    own_order = lax.dynamic_slice_in_dim(ordering, device * (OWN * BS), OWN * BS, 0)
    payload = point_payload(own_order, coordinates, direction, 32)
    own = payload[0]
    plane = exchange(payload, SAME_X)
    half = plane.shape[0] // 2
    same = jnp.where(here_core == 0, plane[:half], plane[half:])
    beyond = [x_around(hop)(same) for hop in (1, 3, 2)]
    total = add_image(own, [plane], jnp.zeros((2 * RHS, OWN * BS), f32))
    others = [to_other_core(piece) for piece in beyond]
    total = add_image(own, beyond, total)
    total = add_image(own, others, total)

    image, near = measure_step(
        lists, valid, gathered, residual, cross, whitening, total, direction
    )
    mine = exchange(image, SAME_CORE)
    other = to_other_core(mine)
    solution_next, residual_next, scaled, back, old = spread_step(
        at, valid, into, self_at, mine, other, near, residual, solution, direction, cross,
        whitening,
    )
    back = back[:PEERS] + to_other_core(back[PEERS:])
    direction_next = sum_step(exchange(back, SAME_CORE), scaled, direction, old)
    return (solution_next, residual_next, direction_next)


def solution(mesh):
    placed = (
        P(),
        P(),
        P(),
        P(("row", "col"), None, None, None),
        P(("row", "col"), None, None),
        P(("row", "col"), None, None),
        P(("row", "col"), None, None),
        P(("row", "col"), None, None),
    )
    return jax.shard_map(
        per_device,
        mesh=mesh,
        in_specs=placed,
        out_specs=(
            P(("row", "col"), None, None),
            P(("row", "col"), None, None),
            P(("row", "col"), None, None),
        ),
        check_vma=False,
    )
```

```python
import functools
import math

import jax
import jax.numpy as jnp
from jax import lax
from jax.experimental import pallas as pl
from jax.experimental.pallas import tpu as pltpu
from jax.sharding import PartitionSpec as P

f32 = jnp.float32
bf16 = jnp.bfloat16
rate = math.sqrt(3.0) / 0.3 * math.log2(math.e)
offset = 1.0 / math.log(2.0)
variance = -0.05 * math.e * math.log(2.0)
nugget = 1.0
AXES = ("row", "col")
BS, RHS, NBR, OWN = 256, 8, 4, 2
HALF = 128
STEP = 4
PEERS = 64
MEGA = 1 << 20


def split2(v):
    top = v.astype(bf16)
    return top, (v - top.astype(f32)).astype(bf16)


def split3(v):
    top = v.astype(bf16).astype(f32)
    rest = v - top
    middle = rest.astype(bf16).astype(f32)
    return top, middle, rest - middle


def pair_dot(a, top, low, dims):
    both = jnp.concatenate(split2(a), axis=0)
    high = lax.dot_general(both, top, (dims, ((), ())), preferred_element_type=f32)
    rest = lax.dot_general(both, low, (dims, ((), ())), preferred_element_type=f32)
    return high[:RHS] + (high[RHS:] + (rest[:RHS] + rest[RHS:]))


def features(place, own):
    a = (place - 0.5) * rate
    norm = jnp.sum(a * a, axis=0, keepdims=True)
    one = jnp.ones_like(norm)
    pad = jnp.zeros((3, norm.shape[1]), f32)
    parts = [-2.0 * a, one, norm, pad] if own else [a, norm, one, pad]
    top, middle, low = split3(jnp.concatenate(parts, axis=0))
    order = [top, middle, top, middle, low, top] if own else [top, top, middle, middle, top, low]
    return jnp.concatenate(order, axis=0).astype(bf16)


def places(tiles, block):
    rows = slice(3 * block, 3 * block + 3)
    return jnp.concatenate([tiles[4, rows, :], tiles[5, rows, :]], axis=1)


def pick_points(order_ref, coordinates_ref, direction_ref, out_ref):
    lane = lax.broadcasted_iota(jnp.int32, (3, HALF), 1)
    groups = 2 * OWN

    def one_point(i, found):
        kept = []
        for group in range(groups):
            at = order_ref[group * HALF + i]
            base = pl.multiple_of((at >> 7) << 7, HALF)
            line = coordinates_ref[:, pl.ds(base, HALF)]
            turned = pltpu.roll(line, (i - (at & (HALF - 1))) & (HALF - 1), 1)
            kept.append(jnp.where(lane == i, turned, found[group]))
        return tuple(kept)

    found = lax.fori_loop(0, HALF, one_point, (jnp.zeros((3, HALF), f32),) * groups, unroll=4)
    pad = jnp.zeros((2, HALF), f32)
    tiles = []
    for block in range(OWN):
        for half in range(2):
            tiles.append(direction_ref[block, :, half * HALF : (half + 1) * HALF])
    for half in range(2):
        tiles.append(jnp.concatenate([found[half], found[2 + half], pad], axis=0))

    def copy(i, carry):
        for part, tile in enumerate(tiles):
            out_ref[i, part] = tile
        return carry

    lax.fori_loop(0, out_ref.shape[0], copy, 0)


def point_payload(own_order, coordinates, direction, copies):
    return pl.pallas_call(
        pick_points,
        out_shape=jax.ShapeDtypeStruct((copies, 6, RHS, HALF), f32),
        in_specs=[
            pl.BlockSpec(memory_space=pltpu.SMEM),
            pl.BlockSpec(memory_space=pltpu.VMEM),
            pl.BlockSpec(memory_space=pltpu.VMEM),
        ],
        out_specs=pl.BlockSpec(memory_space=pltpu.VMEM),
        compiler_params=pltpu.CompilerParams(vmem_limit_bytes=8 * MEGA),
        name="pick_points",
    )(own_order, coordinates, direction)


TALL, WIDE = 512, 256


def image_kernel(pieces, own_ref, start_ref, *refs):
    columns, (out_ref, own_part, column_part, field_part, square) = refs[:pieces], refs[pieces:]
    each = pl.num_programs(0) // pieces

    @pl.when(pl.program_id(0) == 0)
    def _():
        for block in range(OWN):
            own_part[:, block * BS : (block + 1) * BS] = features(places(own_ref, block), True)
        out_ref[...] = start_ref[...]

    def prepare(columns_ref):
        for member in range(STEP):
            for block in range(OWN):
                at = OWN * member + block
                tiles = columns_ref.at[member]
                column_part[at * BS : (at + 1) * BS, :] = features(places(tiles, block), False).T
                field = jnp.concatenate([tiles[2 * block], tiles[2 * block + 1]], axis=1)
                field_part[at] = jnp.concatenate(split2(field * variance), axis=0)

    for index, columns_ref in enumerate(columns):
        pl.when(pl.program_id(0) // each == index)(functools.partial(prepare, columns_ref))
    jobs = [
        (q, r) for r in range(OWN * BS // WIDE) for q in range(STEP * OWN * BS // TALL)
    ]

    def fill(job, slot):
        q, r = jobs[job]
        square[slot] = jnp.dot(
            column_part[q * TALL : (q + 1) * TALL, :],
            own_part[:, r * WIDE : (r + 1) * WIDE],
            preferred_element_type=f32,
        )

    fill(0, 0)
    for job, (q, r) in enumerate(jobs):
        if job + 1 < len(jobs):
            fill(job + 1, (job + 1) % 2)
        for part in range(TALL // BS):
            for lanes in range(WIDE // HALF):
                x = square[
                    job % 2, part * BS : (part + 1) * BS, lanes * HALF : (lanes + 1) * HALF
                ]
                x = jnp.maximum(x, 1e-30)
                u = -offset - x * lax.rsqrt(x)
                tile = u * jnp.exp2(u)
                top, low = split2(tile)
                field = field_part[q * (TALL // BS) + part]
                where = slice(r * WIDE + lanes * HALF, r * WIDE + (lanes + 1) * HALF)
                out_ref[:, where] += jnp.dot(
                    field, top, preferred_element_type=f32
                ) + jnp.dot(field, low, preferred_element_type=f32)


def add_image(own, columns, start):
    pieces, count = len(columns), columns[0].shape[0]
    each = count // STEP
    pairs = pieces * count * OWN * BS * OWN * BS

    def piece_spec(index):
        return pl.BlockSpec(
            (STEP, 6, RHS, HALF),
            lambda i: (jnp.clip(i - index * each, 0, each - 1), 0, 0, 0),
        )

    return pl.pallas_call(
        functools.partial(image_kernel, pieces),
        grid=(pieces * each,),
        in_specs=[
            pl.BlockSpec((6, RHS, HALF), lambda i: (0, 0, 0)),
            pl.BlockSpec((2 * RHS, OWN * BS), lambda i: (0, 0)),
        ]
        + [piece_spec(index) for index in range(pieces)],
        out_specs=pl.BlockSpec((2 * RHS, OWN * BS), lambda i: (0, 0)),
        out_shape=jax.ShapeDtypeStruct((2 * RHS, OWN * BS), f32),
        scratch_shapes=[
            pltpu.VMEM((48, OWN * BS), bf16),
            pltpu.VMEM((STEP * OWN * BS, 48), bf16),
            pltpu.VMEM((OWN * STEP, 2 * RHS, BS), bf16),
            pltpu.VMEM((2, TALL, WIDE), f32),
        ],
        compiler_params=pltpu.CompilerParams(vmem_limit_bytes=24 * MEGA),
        cost_estimate=pl.CostEstimate(
            flops=600 * pairs, transcendentals=2 * pairs, bytes_accessed=pieces * count * 6 * 4096
        ),
        name="image",
    )(own, start, *columns)


def split_kernel(cross_ref, whitening_ref, cross_top, cross_low, whiten_top, whiten_low):
    def one(at, carry):
        cross_top[at], cross_low[at] = split2(cross_ref[at])
        return carry

    lax.fori_loop(0, OWN * NBR, one, 0)
    rows = lax.broadcasted_iota(jnp.int32, (BS, BS), 0)
    lanes = lax.broadcasted_iota(jnp.int32, (BS, BS), 1)
    for b in range(OWN):
        whiten = whitening_ref[b] + jnp.where(rows == lanes, 1.0, 0.0)
        whiten_top[b], whiten_low[b] = split2(whiten)


def split_factors(cross, whitening):
    vmem = pl.BlockSpec(memory_space=pltpu.VMEM)
    shapes = [(OWN * NBR, BS, BS)] * 2 + [(OWN, BS, BS)] * 2
    return pl.pallas_call(
        split_kernel,
        out_shape=tuple(jax.ShapeDtypeStruct(shape, bf16) for shape in shapes),
        in_specs=[vmem] * 2,
        out_specs=(vmem,) * 4,
        compiler_params=pltpu.CompilerParams(vmem_limit_bytes=12 * MEGA),
        cost_estimate=pl.CostEstimate(flops=4 << 20, transcendentals=0, bytes_accessed=5 << 20),
        name="split_factors",
    )(cross.reshape(OWN * NBR, BS, BS), whitening)


def lower(near, valid_ref, cross_top, cross_low, field, block):
    total = field
    for k in range(NBR):
        at = block * NBR + k
        weight = valid_ref[at].astype(f32)
        total = total - pair_dot(
            near(at) * weight, cross_top[at], cross_low[at], ((1,), (1,))
        )
    return total


def lanes_of(v):
    return v[:, :HALF] + v[:, HALF:]


def measure_kernel(
    list_ref, valid_ref, all_ref, residual_ref, cross_top, cross_low, whiten_top, whiten_low,
    sum_ref, direction_ref,
    out_ref, near_ref, near_buf, sems,
):
    copies = []
    for b in range(OWN):
        for k in range(NBR):
            at = b * NBR + k
            copies.append(
                pltpu.make_async_copy(all_ref.at[list_ref[at]], near_buf.at[at], sems.at[at])
            )
            copies[-1].start()
    for copy in copies:
        copy.wait()
    old = jnp.zeros((RHS, HALF), f32)
    curvature = jnp.zeros((RHS, HALF), f32)
    tiles = []
    for b in range(OWN):
        lowered = lower(
            lambda at: near_buf[at], valid_ref, cross_top, cross_low, residual_ref[b], b
        )
        mapped = pair_dot(lowered, whiten_top[b], whiten_low[b], ((1,), (1,)))
        old = old + lanes_of(mapped * mapped)
        here = slice(b * BS, (b + 1) * BS)
        image = sum_ref[:RHS, here] + sum_ref[RHS:, here] + nugget * direction_ref[b]
        curvature = curvature + lanes_of(direction_ref[b] * image)
        tiles += [image[:, :HALF], image[:, HALF:]]
    lane = lax.broadcasted_iota(jnp.int32, (RHS, HALF), 1)
    old = jnp.sum(old, axis=1, keepdims=True)
    curvature = jnp.sum(curvature, axis=1, keepdims=True)
    tiles.append(jnp.where(lane == 0, old, jnp.where(lane == 1, curvature, 0.0)))

    def copy(i, carry):
        for part, tile in enumerate(tiles):
            out_ref[i, part] = tile
        return carry

    lax.fori_loop(0, out_ref.shape[0], copy, 0)
    near_ref[...] = near_buf[...]


def measure_step(lists, valid, gathered, residual, factors, total, direction):
    smem = pl.BlockSpec(memory_space=pltpu.SMEM)
    vmem = pl.BlockSpec(memory_space=pltpu.VMEM)
    return pl.pallas_call(
        measure_kernel,
        out_shape=(
            jax.ShapeDtypeStruct((PEERS, 5, RHS, HALF), f32),
            jax.ShapeDtypeStruct((OWN * NBR, RHS, BS), f32),
        ),
        in_specs=[smem, smem, pl.BlockSpec(memory_space=pl.ANY)] + [vmem] * 7,
        out_specs=(vmem, vmem),
        scratch_shapes=[
            pltpu.VMEM((OWN * NBR, RHS, BS), f32),
            pltpu.SemaphoreType.DMA((OWN * NBR,)),
        ],
        compiler_params=pltpu.CompilerParams(vmem_limit_bytes=24 * MEGA),
        name="measure_step",
    )(lists, valid, gathered, residual, *factors, total, direction)


def spread_kernel(
    at_ref, valid_ref, into_ref, self_ref, mine_ref, other_ref, near_ref, residual_ref, solution_ref,
    direction_ref, cross_top, cross_low, whiten_top, whiten_low,
    solution_out, residual_out, scaled_out, out_ref, old_out,
):
    total = jnp.zeros((RHS, HALF), f32)
    for i in range(PEERS):
        total = total + mine_ref[i, 4] + other_ref[i, 4]
    old = total[:, 0:1]
    step = old / total[:, 1:2]

    def clear(i, carry):
        for part in range(2 * OWN):
            out_ref[i, part] = jnp.zeros((RHS, HALF), f32)
        return carry

    lax.fori_loop(0, 2 * PEERS, clear, 0)

    def image_of(at):
        slot = at & 63
        a = jnp.concatenate([mine_ref[slot, 2 * (at >> 7)], mine_ref[slot, 2 * (at >> 7) + 1]], 1)
        b = jnp.concatenate([other_ref[slot, 2 * (at >> 7)], other_ref[slot, 2 * (at >> 7) + 1]], 1)
        return jnp.where(((at >> 6) & 1) == 0, a, b)

    newer = jnp.zeros((RHS, HALF), f32)
    for b in range(OWN):
        solution_out[b] = solution_ref[b] + step * direction_ref[b]
        image = jnp.concatenate(
            [mine_ref[self_ref[0], 2 * b], mine_ref[self_ref[0], 2 * b + 1]], 1
        )
        following = residual_ref[b] - step * image
        residual_out[b] = following
        lowered = lower(
            lambda at: near_ref[at] - step * image_of(at_ref[at]),
            valid_ref, cross_top, cross_low, following, b,
        )
        mapped = pair_dot(lowered, whiten_top[b], whiten_low[b], ((1,), (1,)))
        newer = newer + lanes_of(mapped * mapped)
        scaled = pair_dot(mapped, whiten_top[b], whiten_low[b], ((1,), (0,)))
        scaled_out[b] = scaled
        for k in range(NBR):
            at = b * NBR + k
            spread = pair_dot(scaled, cross_top[at], cross_low[at], ((1,), (0,)))
            spread = spread * valid_ref[at].astype(f32)
            to = into_ref[at]
            out_ref[to >> 1, 2 * (to & 1)] += spread[:, :HALF]
            out_ref[to >> 1, 2 * (to & 1) + 1] += spread[:, HALF:]
    newer = jnp.sum(newer, axis=1, keepdims=True)
    lane = lax.broadcasted_iota(jnp.int32, (RHS, HALF), 1)
    newer = jnp.where(lane == 0, newer, 0.0)

    def share(i, carry):
        out_ref[i, 2 * OWN] = newer
        return carry

    lax.fori_loop(0, 2 * PEERS, share, 0)
    old_out[...] = jnp.broadcast_to(old, (RHS, HALF))


def sum_kernel(all_ref, scaled_ref, direction_ref, old_ref, out_ref):
    total = all_ref[0]
    for i in range(1, PEERS):
        total = total + all_ref[i]
    ratio = total[2 * OWN, :, 0:1] / old_ref[:, 0:1]
    for b in range(OWN):
        back = jnp.concatenate([total[2 * b], total[2 * b + 1]], axis=1)
        out_ref[b] = scaled_ref[b] - back + ratio * direction_ref[b]


def sum_step(everything, scaled, direction, old):
    vmem = pl.BlockSpec(memory_space=pltpu.VMEM)
    return pl.pallas_call(
        sum_kernel,
        out_shape=jax.ShapeDtypeStruct((OWN, RHS, BS), f32),
        in_specs=[vmem] * 4,
        out_specs=vmem,
        compiler_params=pltpu.CompilerParams(vmem_limit_bytes=8 * MEGA),
        name="sum_step",
    )(everything, scaled, direction, old)


def spread_step(
    at, valid, into, self_at, mine, other, near, residual, solution, direction, factors
):
    smem = pl.BlockSpec(memory_space=pltpu.SMEM)
    vmem = pl.BlockSpec(memory_space=pltpu.VMEM)
    own = jax.ShapeDtypeStruct((OWN, RHS, BS), f32)
    return pl.pallas_call(
        spread_kernel,
        out_shape=(
            own,
            own,
            own,
            jax.ShapeDtypeStruct((2 * PEERS, 2 * OWN + 1, RHS, HALF), f32),
            jax.ShapeDtypeStruct((RHS, HALF), f32),
        ),
        in_specs=[smem] * 4 + [vmem] * 10,
        out_specs=(vmem,) * 5,
        compiler_params=pltpu.CompilerParams(vmem_limit_bytes=40 * MEGA),
        name="spread_step",
    )(
        at, valid, into, self_at, mine, other, near, residual, solution, direction, *factors
    )


def x_around(hop):
    def target(i):
        return (i // 8 + hop) % 4 * 8 + i % 8

    return functools.partial(
        lax.ppermute, axis_name="col", perm=[(i, target(i)) for i in range(32)]
    )


def to_other_core(value):
    return lax.ppermute(value, "col", [(i, i ^ 1) for i in range(32)])


def exchange(value, groups):
    return lax.all_to_all(value, AXES, 0, 0, axis_index_groups=groups, tiled=True)


SAME_CORE = [[2 * j + core for j in range(PEERS)] for core in range(2)]
SAME_X_CORE = [
    [y * 32 + x * 8 + z * 2 + core for y in range(4) for z in range(4)]
    for x in range(4)
    for core in range(2)
]


def per_device(coordinates, ordering, neighbours, cross, whitening, solution, residual, direction):
    row = lax.axis_index("row")
    col = lax.axis_index("col")
    device = row * 32 + col
    here_core = device % 2
    own_ids = device * OWN + jnp.arange(OWN, dtype=jnp.int32)
    own_lists = lax.dynamic_slice_in_dim(neighbours, device * OWN, OWN, 0)
    valid = (own_lists < own_ids[:, None]).astype(jnp.int32).reshape(-1)
    lists = own_lists.reshape(-1)
    their = lists // OWN
    core_gap = (their % 2) ^ here_core
    at = ((lists % OWN) * 2 + core_gap) * PEERS + their // 2
    into = (core_gap * PEERS + their // 2) * OWN + lists % OWN
    self_at = (device // 2)[None]

    gathered = lax.all_gather(residual, AXES, axis=0, tiled=True)

    own_order = lax.dynamic_slice_in_dim(ordering, device * (OWN * BS), OWN * BS, 0)
    factors = split_factors(cross, whitening)
    payload = point_payload(own_order, coordinates, direction, 16)
    own = payload[0]
    plane = exchange(payload, SAME_X_CORE)
    plane, plane_other = lax.optimization_barrier((plane, to_other_core(plane)))
    beyond = [x_around(hop)(plane) for hop in (1, 3, 2)]
    total = add_image(own, [plane, plane_other], jnp.zeros((2 * RHS, OWN * BS), f32))
    others = [to_other_core(piece) for piece in beyond]
    total = add_image(own, beyond, total)
    total = add_image(own, others, total)

    image, near = measure_step(lists, valid, gathered, residual, factors, total, direction)
    mine = exchange(image, SAME_CORE)
    other = to_other_core(mine)
    solution_next, residual_next, scaled, back, old = spread_step(
        at, valid, into, self_at, mine, other, near, residual, solution, direction, factors
    )
    back = back[:PEERS] + to_other_core(back[PEERS:])
    direction_next = sum_step(exchange(back, SAME_CORE), scaled, direction, old)
    return (solution_next, residual_next, direction_next)


def solution(mesh):
    placed = (
        P(),
        P(),
        P(),
        P(("row", "col"), None, None, None),
        P(("row", "col"), None, None),
        P(("row", "col"), None, None),
        P(("row", "col"), None, None),
        P(("row", "col"), None, None),
    )
    return jax.shard_map(
        per_device,
        mesh=mesh,
        in_specs=placed,
        out_specs=(
            P(("row", "col"), None, None),
            P(("row", "col"), None, None),
            P(("row", "col"), None, None),
        ),
        check_vma=False,
    )
```

```python
import functools
import math

import jax
import jax.numpy as jnp
from jax import lax
from jax.experimental import pallas as pl
from jax.experimental.pallas import tpu as pltpu
from jax.sharding import PartitionSpec as P

f32 = jnp.float32
bf16 = jnp.bfloat16
rate = math.sqrt(3.0) / 0.3 * math.log2(math.e)
offset = 1.0 / math.log(2.0)
variance = -0.05 * math.e * math.log(2.0)
nugget = 1.0
AXES = ("row", "col")
BS, RHS, NBR, OWN = 256, 8, 4, 2
HALF = 128
STEP = 4
PEERS = 64
PAIR = 2 * OWN * BS
MEGA = 1 << 20


def split2(v):
    top = v.astype(bf16)
    return top, (v - top.astype(f32)).astype(bf16)


def split3(v):
    top = v.astype(bf16).astype(f32)
    rest = v - top
    middle = rest.astype(bf16).astype(f32)
    return top, middle, rest - middle


def pair_dot(a, top, low, dims):
    both = jnp.concatenate(split2(a), axis=0)
    high = lax.dot_general(both, top, (dims, ((), ())), preferred_element_type=f32)
    rest = lax.dot_general(both, low, (dims, ((), ())), preferred_element_type=f32)
    return high[:RHS] + (high[RHS:] + (rest[:RHS] + rest[RHS:]))


def features(place, own):
    a = (place - 0.5) * rate
    norm = jnp.sum(a * a, axis=0, keepdims=True)
    one = jnp.ones_like(norm)
    pad = jnp.zeros((3, norm.shape[1]), f32)
    parts = [-2.0 * a, one, norm, pad] if own else [a, norm, one, pad]
    top, middle, low = split3(jnp.concatenate(parts, axis=0))
    order = [top, middle, top, middle, low, top] if own else [top, top, middle, middle, top, low]
    return jnp.concatenate(order, axis=0).astype(bf16)


def places(tiles, block):
    rows = slice(3 * block, 3 * block + 3)
    return jnp.concatenate([tiles[4, rows, :], tiles[5, rows, :]], axis=1)


def pick_points(
    all_order, all_coordinates, direction_ref, out_ref, order_ref, coordinates_ref, sems
):
    device = lax.axis_index("row") * 32 + lax.axis_index("col")
    pair = pl.multiple_of(device // 2 * PAIR, PAIR)
    order_copy = pltpu.make_async_copy(all_order.at[pl.ds(pair, PAIR)], order_ref, sems.at[0])
    order_copy.start()
    copy_points = pltpu.make_async_copy(all_coordinates, coordinates_ref, sems.at[1])
    copy_points.start()
    order_copy.wait()
    copy_points.wait()
    first = device % 2 * (OWN * BS)
    lane = lax.broadcasted_iota(jnp.int32, (3, HALF), 1)
    groups = 2 * OWN

    def one_point(i, found):
        kept = []
        for group in range(groups):
            at = order_ref[first + group * HALF + i]
            base = pl.multiple_of((at >> 7) << 7, HALF)
            line = coordinates_ref[:, pl.ds(base, HALF)]
            turned = pltpu.roll(line, (i - (at & (HALF - 1))) & (HALF - 1), 1)
            kept.append(jnp.where(lane == i, turned, found[group]))
        return tuple(kept)

    found = lax.fori_loop(0, HALF, one_point, (jnp.zeros((3, HALF), f32),) * groups, unroll=16)
    pad = jnp.zeros((2, HALF), f32)
    tiles = []
    for block in range(OWN):
        for half in range(2):
            tiles.append(direction_ref[block, :, half * HALF : (half + 1) * HALF])
    for half in range(2):
        tiles.append(jnp.concatenate([found[half], found[2 + half], pad], axis=0))

    def copy(i, carry):
        for part, tile in enumerate(tiles):
            out_ref[i, part] = tile
        return carry

    lax.fori_loop(0, out_ref.shape[0], copy, 0)


def point_payload(ordering, coordinates, direction, copies):
    return pl.pallas_call(
        pick_points,
        out_shape=jax.ShapeDtypeStruct((copies, 6, RHS, HALF), f32),
        in_specs=[
            pl.BlockSpec(memory_space=pltpu.HBM),
            pl.BlockSpec(memory_space=pltpu.HBM),
            pl.BlockSpec(memory_space=pltpu.VMEM),
        ],
        out_specs=pl.BlockSpec(memory_space=pltpu.VMEM),
        scratch_shapes=[
            pltpu.SMEM((PAIR,), jnp.int32),
            pltpu.VMEM(coordinates.shape, f32),
            pltpu.SemaphoreType.DMA((2,)),
        ],
        compiler_params=pltpu.CompilerParams(vmem_limit_bytes=56 * MEGA),
        name="pick_points",
    )(ordering, coordinates, direction)


TALL, WIDE = 512, 256


def image_kernel(pieces, own_ref, start_ref, *refs):
    columns, (out_ref, own_part, column_part, field_part, square) = refs[:pieces], refs[pieces:]
    each = pl.num_programs(0) // pieces

    @pl.when(pl.program_id(0) == 0)
    def _():
        for block in range(OWN):
            own_part[:, block * BS : (block + 1) * BS] = features(places(own_ref, block), True)
        out_ref[...] = start_ref[...]

    def prepare(columns_ref):
        for member in range(STEP):
            for block in range(OWN):
                at = OWN * member + block
                tiles = columns_ref.at[member]
                column_part[at * BS : (at + 1) * BS, :] = features(places(tiles, block), False).T
                field = jnp.concatenate([tiles[2 * block], tiles[2 * block + 1]], axis=1)
                field_part[at] = jnp.concatenate(split2(field * variance), axis=0)

    for index, columns_ref in enumerate(columns):
        pl.when(pl.program_id(0) // each == index)(functools.partial(prepare, columns_ref))
    jobs = [
        (q, r) for r in range(OWN * BS // WIDE) for q in range(STEP * OWN * BS // TALL)
    ]

    def fill(job, slot):
        q, r = jobs[job]
        square[slot] = jnp.dot(
            column_part[q * TALL : (q + 1) * TALL, :],
            own_part[:, r * WIDE : (r + 1) * WIDE],
            preferred_element_type=f32,
        )

    fill(0, 0)
    for job, (q, r) in enumerate(jobs):
        if job + 1 < len(jobs):
            fill(job + 1, (job + 1) % 2)
        for part in range(TALL // BS):
            for lanes in range(WIDE // HALF):
                x = square[
                    job % 2, part * BS : (part + 1) * BS, lanes * HALF : (lanes + 1) * HALF
                ]
                x = jnp.maximum(x, 1e-30)
                u = -offset - x * lax.rsqrt(x)
                tile = u * jnp.exp2(u)
                top, low = split2(tile)
                field = field_part[q * (TALL // BS) + part]
                where = slice(r * WIDE + lanes * HALF, r * WIDE + (lanes + 1) * HALF)
                out_ref[:, where] += jnp.dot(
                    field, top, preferred_element_type=f32
                ) + jnp.dot(field, low, preferred_element_type=f32)


def add_image(own, columns, start):
    pieces, count = len(columns), columns[0].shape[0]
    each = count // STEP
    pairs = pieces * count * OWN * BS * OWN * BS

    def piece_spec(index):
        return pl.BlockSpec(
            (STEP, 6, RHS, HALF),
            lambda i: (jnp.clip(i - index * each, 0, each - 1), 0, 0, 0),
        )

    return pl.pallas_call(
        functools.partial(image_kernel, pieces),
        grid=(pieces * each,),
        in_specs=[
            pl.BlockSpec((6, RHS, HALF), lambda i: (0, 0, 0)),
            pl.BlockSpec((2 * RHS, OWN * BS), lambda i: (0, 0)),
        ]
        + [piece_spec(index) for index in range(pieces)],
        out_specs=pl.BlockSpec((2 * RHS, OWN * BS), lambda i: (0, 0)),
        out_shape=jax.ShapeDtypeStruct((2 * RHS, OWN * BS), f32),
        scratch_shapes=[
            pltpu.VMEM((48, OWN * BS), bf16),
            pltpu.VMEM((STEP * OWN * BS, 48), bf16),
            pltpu.VMEM((OWN * STEP, 2 * RHS, BS), bf16),
            pltpu.VMEM((2, TALL, WIDE), f32),
        ],
        compiler_params=pltpu.CompilerParams(vmem_limit_bytes=10 * MEGA),
        cost_estimate=pl.CostEstimate(
            flops=600 * pairs, transcendentals=2 * pairs, bytes_accessed=pieces * count * 6 * 4096
        ),
        name="image",
    )(own, start, *columns)


def split_whitening(whitening_ref, whiten_top, whiten_low):
    rows = lax.broadcasted_iota(jnp.int32, (BS, BS), 0)
    lanes = lax.broadcasted_iota(jnp.int32, (BS, BS), 1)
    for b in range(OWN):
        whiten = whitening_ref[b] + jnp.where(rows == lanes, 1.0, 0.0)
        whiten_top[b], whiten_low[b] = split2(whiten)


def split_kernel(cross_ref, cross_top, cross_low):
    def one(at, carry):
        cross_top[at], cross_low[at] = split2(cross_ref[at])
        return carry

    lax.fori_loop(0, OWN * NBR, one, 0)


def split_factors(cross):
    vmem = pl.BlockSpec(memory_space=pltpu.VMEM)
    return pl.pallas_call(
        split_kernel,
        out_shape=(jax.ShapeDtypeStruct((OWN * NBR, BS, BS), bf16),) * 2,
        in_specs=[vmem],
        out_specs=(vmem,) * 2,
        compiler_params=pltpu.CompilerParams(vmem_limit_bytes=12 * MEGA),
        cost_estimate=pl.CostEstimate(flops=4 << 20, transcendentals=0, bytes_accessed=5 << 20),
        name="split_factors",
    )(cross.reshape(OWN * NBR, BS, BS))


def lower(near, valid_ref, cross_top, cross_low, field, block):
    total = field
    for k in range(NBR):
        at = block * NBR + k
        weight = valid_ref[at].astype(f32)
        total = total - pair_dot(
            near(at) * weight, cross_top[at], cross_low[at], ((1,), (1,))
        )
    return total


def lanes_of(v):
    return v[:, :HALF] + v[:, HALF:]


def measure_kernel(
    list_ref, valid_ref, all_ref, residual_ref, cross_top, cross_low, whitening_ref,
    sum_ref, direction_ref,
    out_ref, near_ref, near_buf, whiten_top, whiten_low, sems,
):
    copies = []
    for b in range(OWN):
        for k in range(NBR):
            at = b * NBR + k
            copies.append(
                pltpu.make_async_copy(all_ref.at[list_ref[at]], near_buf.at[at], sems.at[at])
            )
            copies[-1].start()
    split_whitening(whitening_ref, whiten_top, whiten_low)
    for copy in copies:
        copy.wait()
    old = jnp.zeros((RHS, HALF), f32)
    curvature = jnp.zeros((RHS, HALF), f32)
    tiles = []
    for b in range(OWN):
        lowered = lower(
            lambda at: near_buf[at], valid_ref, cross_top, cross_low, residual_ref[b], b
        )
        mapped = pair_dot(lowered, whiten_top[b], whiten_low[b], ((1,), (1,)))
        old = old + lanes_of(mapped * mapped)
        here = slice(b * BS, (b + 1) * BS)
        image = sum_ref[:RHS, here] + sum_ref[RHS:, here] + nugget * direction_ref[b]
        curvature = curvature + lanes_of(direction_ref[b] * image)
        tiles += [image[:, :HALF], image[:, HALF:]]
    lane = lax.broadcasted_iota(jnp.int32, (RHS, HALF), 1)
    old = jnp.sum(old, axis=1, keepdims=True)
    curvature = jnp.sum(curvature, axis=1, keepdims=True)
    tiles.append(jnp.where(lane == 0, old, jnp.where(lane == 1, curvature, 0.0)))

    def copy(i, carry):
        for part, tile in enumerate(tiles):
            out_ref[i, part] = tile
        return carry

    lax.fori_loop(0, out_ref.shape[0], copy, 0)
    near_ref[...] = near_buf[...]


def measure_step(lists, valid, gathered, residual, factors, total, direction):
    smem = pl.BlockSpec(memory_space=pltpu.SMEM)
    vmem = pl.BlockSpec(memory_space=pltpu.VMEM)
    return pl.pallas_call(
        measure_kernel,
        out_shape=(
            jax.ShapeDtypeStruct((PEERS, 5, RHS, HALF), f32),
            jax.ShapeDtypeStruct((OWN * NBR, RHS, BS), f32),
        ),
        in_specs=[smem, smem, pl.BlockSpec(memory_space=pl.ANY)] + [vmem] * 6,
        out_specs=(vmem, vmem),
        scratch_shapes=[
            pltpu.VMEM((OWN * NBR, RHS, BS), f32),
            pltpu.VMEM((OWN, BS, BS), bf16),
            pltpu.VMEM((OWN, BS, BS), bf16),
            pltpu.SemaphoreType.DMA((OWN * NBR,)),
        ],
        compiler_params=pltpu.CompilerParams(vmem_limit_bytes=8 * MEGA),
        name="measure_step",
    )(lists, valid, gathered, residual, *factors, total, direction)


def spread_kernel(
    at_ref, valid_ref, into_ref, self_ref, mine_ref, other_ref, near_ref, residual_ref, solution_ref,
    direction_ref, cross_top, cross_low, whitening_ref,
    solution_out, residual_out, scaled_out, out_ref, old_out,
    whiten_top, whiten_low,
):
    split_whitening(whitening_ref, whiten_top, whiten_low)
    total = jnp.zeros((RHS, HALF), f32)
    for i in range(PEERS):
        total = total + mine_ref[i, 4] + other_ref[i, 4]
    old = total[:, 0:1]
    step = old / total[:, 1:2]

    def clear(i, carry):
        for part in range(2 * OWN):
            out_ref[i, part] = jnp.zeros((RHS, HALF), f32)
        return carry

    lax.fori_loop(0, 2 * PEERS, clear, 0)

    def image_of(at):
        slot = at & 63
        a = jnp.concatenate([mine_ref[slot, 2 * (at >> 7)], mine_ref[slot, 2 * (at >> 7) + 1]], 1)
        b = jnp.concatenate([other_ref[slot, 2 * (at >> 7)], other_ref[slot, 2 * (at >> 7) + 1]], 1)
        return jnp.where(((at >> 6) & 1) == 0, a, b)

    newer = jnp.zeros((RHS, HALF), f32)
    for b in range(OWN):
        solution_out[b] = solution_ref[b] + step * direction_ref[b]
        image = jnp.concatenate(
            [mine_ref[self_ref[0], 2 * b], mine_ref[self_ref[0], 2 * b + 1]], 1
        )
        following = residual_ref[b] - step * image
        residual_out[b] = following
        lowered = lower(
            lambda at: near_ref[at] - step * image_of(at_ref[at]),
            valid_ref, cross_top, cross_low, following, b,
        )
        mapped = pair_dot(lowered, whiten_top[b], whiten_low[b], ((1,), (1,)))
        newer = newer + lanes_of(mapped * mapped)
        scaled = pair_dot(mapped, whiten_top[b], whiten_low[b], ((1,), (0,)))
        scaled_out[b] = scaled
        for k in range(NBR):
            at = b * NBR + k
            spread = pair_dot(scaled, cross_top[at], cross_low[at], ((1,), (0,)))
            spread = spread * valid_ref[at].astype(f32)
            to = into_ref[at]
            out_ref[to >> 1, 2 * (to & 1)] += spread[:, :HALF]
            out_ref[to >> 1, 2 * (to & 1) + 1] += spread[:, HALF:]
    newer = jnp.sum(newer, axis=1, keepdims=True)
    lane = lax.broadcasted_iota(jnp.int32, (RHS, HALF), 1)
    newer = jnp.where(lane == 0, newer, 0.0)

    def share(i, carry):
        out_ref[i, 2 * OWN] = newer
        return carry

    lax.fori_loop(0, 2 * PEERS, share, 0)
    old_out[...] = jnp.broadcast_to(old, (RHS, HALF))


def sum_kernel(all_ref, scaled_ref, direction_ref, old_ref, out_ref):
    total = all_ref[0]
    for i in range(1, PEERS):
        total = total + all_ref[i]
    ratio = total[2 * OWN, :, 0:1] / old_ref[:, 0:1]
    for b in range(OWN):
        back = jnp.concatenate([total[2 * b], total[2 * b + 1]], axis=1)
        out_ref[b] = scaled_ref[b] - back + ratio * direction_ref[b]


def sum_step(everything, scaled, direction, old):
    vmem = pl.BlockSpec(memory_space=pltpu.VMEM)
    return pl.pallas_call(
        sum_kernel,
        out_shape=jax.ShapeDtypeStruct((OWN, RHS, BS), f32),
        in_specs=[vmem] * 4,
        out_specs=vmem,
        compiler_params=pltpu.CompilerParams(vmem_limit_bytes=8 * MEGA),
        name="sum_step",
    )(everything, scaled, direction, old)


def spread_step(
    at, valid, into, self_at, mine, other, near, residual, solution, direction, factors
):
    smem = pl.BlockSpec(memory_space=pltpu.SMEM)
    vmem = pl.BlockSpec(memory_space=pltpu.VMEM)
    own = jax.ShapeDtypeStruct((OWN, RHS, BS), f32)
    return pl.pallas_call(
        spread_kernel,
        out_shape=(
            own,
            own,
            own,
            jax.ShapeDtypeStruct((2 * PEERS, 2 * OWN + 1, RHS, HALF), f32),
            jax.ShapeDtypeStruct((RHS, HALF), f32),
        ),
        in_specs=[smem] * 4 + [vmem] * 9,
        out_specs=(vmem,) * 5,
        scratch_shapes=[
            pltpu.VMEM((OWN, BS, BS), bf16),
            pltpu.VMEM((OWN, BS, BS), bf16),
        ],
        compiler_params=pltpu.CompilerParams(vmem_limit_bytes=16 * MEGA),
        name="spread_step",
    )(
        at, valid, into, self_at, mine, other, near, residual, solution, direction, *factors
    )


def x_around(hop):
    def target(i):
        return (i // 8 + hop) % 4 * 8 + i % 8

    return functools.partial(
        lax.ppermute, axis_name="col", perm=[(i, target(i)) for i in range(32)]
    )


def to_other_core(value):
    return lax.ppermute(value, "col", [(i, i ^ 1) for i in range(32)])


def exchange(value, groups):
    return lax.all_to_all(value, AXES, 0, 0, axis_index_groups=groups, tiled=True)


SAME_CORE = [[2 * j + core for j in range(PEERS)] for core in range(2)]
SAME_X_CORE = [
    [y * 32 + x * 8 + z * 2 + core for y in range(4) for z in range(4)]
    for x in range(4)
    for core in range(2)
]


def per_device(coordinates, ordering, neighbours, cross, whitening, solution, residual, direction):
    row = lax.axis_index("row")
    col = lax.axis_index("col")
    device = row * 32 + col
    here_core = device % 2
    own_ids = device * OWN + jnp.arange(OWN, dtype=jnp.int32)
    own_lists = lax.dynamic_slice_in_dim(neighbours, device * OWN, OWN, 0)
    valid = (own_lists < own_ids[:, None]).astype(jnp.int32).reshape(-1)
    lists = own_lists.reshape(-1)
    their = lists // OWN
    core_gap = (their % 2) ^ here_core
    at = ((lists % OWN) * 2 + core_gap) * PEERS + their // 2
    into = (core_gap * PEERS + their // 2) * OWN + lists % OWN
    self_at = (device // 2)[None]

    gathered = lax.all_gather(residual, AXES, axis=0, tiled=True)

    factors = (*split_factors(cross), whitening)
    payload = point_payload(ordering, coordinates, direction, 16)
    own = payload[0]
    plane = exchange(payload, SAME_X_CORE)
    plane, plane_other = lax.optimization_barrier((plane, to_other_core(plane)))
    beyond = [x_around(hop)(plane) for hop in (1, 3, 2)]
    total = add_image(own, [plane, plane_other], jnp.zeros((2 * RHS, OWN * BS), f32))
    others = [to_other_core(piece) for piece in beyond]
    total = add_image(own, beyond, total)
    total, gathered = lax.optimization_barrier((total, gathered))
    total = add_image(own, others, total)

    image, near = measure_step(lists, valid, gathered, residual, factors, total, direction)
    mine = exchange(image, SAME_CORE)
    other = to_other_core(mine)
    solution_next, residual_next, scaled, back, old = spread_step(
        at, valid, into, self_at, mine, other, near, residual, solution, direction, factors
    )
    back = back[:PEERS] + to_other_core(back[PEERS:])
    direction_next = sum_step(exchange(back, SAME_CORE), scaled, direction, old)
    return (solution_next, residual_next, direction_next)


def solution(mesh):
    placed = (
        P(),
        P(),
        P(),
        P(("row", "col"), None, None, None),
        P(("row", "col"), None, None),
        P(("row", "col"), None, None),
        P(("row", "col"), None, None),
        P(("row", "col"), None, None),
    )
    return jax.shard_map(
        per_device,
        mesh=mesh,
        in_specs=placed,
        out_specs=(
            P(("row", "col"), None, None),
            P(("row", "col"), None, None),
            P(("row", "col"), None, None),
        ),
        check_vma=False,
    )
```

```python
import functools
import math

import jax
import jax.numpy as jnp
from jax import lax
from jax.experimental import pallas as pl
from jax.experimental.pallas import tpu as pltpu
from jax.sharding import PartitionSpec as P

f32 = jnp.float32
bf16 = jnp.bfloat16
rate = math.sqrt(3.0) / 0.3 * math.log2(math.e)
offset = 1.0 / math.log(2.0)
variance = -0.05 * math.e * math.log(2.0)
nugget = 1.0
AXES = ("row", "col")
BS, RHS, NBR, OWN = 256, 8, 4, 2
HALF = 128
STEP = 4
PEERS = 64
PAIR = 2 * OWN * BS
MEGA = 1 << 20


def split2(v):
    top = v.astype(bf16)
    return top, (v - top.astype(f32)).astype(bf16)


def split3(v):
    top = v.astype(bf16).astype(f32)
    rest = v - top
    middle = rest.astype(bf16).astype(f32)
    return top, middle, rest - middle


def pair_dot(a, top, low, dims):
    both = jnp.concatenate(split2(a), axis=0)
    high = lax.dot_general(both, top, (dims, ((), ())), preferred_element_type=f32)
    rest = lax.dot_general(both, low, (dims, ((), ())), preferred_element_type=f32)
    return high[:RHS] + (high[RHS:] + (rest[:RHS] + rest[RHS:]))


def features(place, own):
    a = (place - 0.5) * rate
    norm = jnp.sum(a * a, axis=0, keepdims=True)
    one = jnp.ones_like(norm)
    pad = jnp.zeros((3, norm.shape[1]), f32)
    parts = [-2.0 * a, one, norm, pad] if own else [a, norm, one, pad]
    top, middle, low = split3(jnp.concatenate(parts, axis=0))
    order = [top, middle, top, middle, low, top] if own else [top, top, middle, middle, top, low]
    return jnp.concatenate(order, axis=0).astype(bf16)


def places(tiles, block):
    rows = slice(3 * block, 3 * block + 3)
    return jnp.concatenate([tiles[4, rows, :], tiles[5, rows, :]], axis=1)


def pick_points(
    all_order, all_coordinates, direction_ref, out_ref, own_ref, order_ref, coordinates_ref, sems
):
    device = lax.axis_index("row") * 32 + lax.axis_index("col")
    pair = pl.multiple_of(device // 2 * PAIR, PAIR)
    order_copy = pltpu.make_async_copy(all_order.at[pl.ds(pair, PAIR)], order_ref, sems.at[0])
    order_copy.start()
    copy_points = pltpu.make_async_copy(all_coordinates, coordinates_ref, sems.at[1])
    copy_points.start()
    order_copy.wait()
    copy_points.wait()
    first = device % 2 * (OWN * BS)
    lane = lax.broadcasted_iota(jnp.int32, (3, HALF), 1)
    groups = 2 * OWN

    def one_point(i, found):
        kept = []
        for group in range(groups):
            at = order_ref[first + group * HALF + i]
            base = pl.multiple_of((at >> 7) << 7, HALF)
            line = coordinates_ref[:, pl.ds(base, HALF)]
            turned = pltpu.roll(line, (i - (at & (HALF - 1))) & (HALF - 1), 1)
            kept.append(jnp.where(lane == i, turned, found[group]))
        return tuple(kept)

    found = lax.fori_loop(0, HALF, one_point, (jnp.zeros((3, HALF), f32),) * groups, unroll=16)
    pad = jnp.zeros((2, HALF), f32)
    tiles = []
    for block in range(OWN):
        for half in range(2):
            tiles.append(direction_ref[block, :, half * HALF : (half + 1) * HALF])
    for half in range(2):
        tiles.append(jnp.concatenate([found[half], found[2 + half], pad], axis=0))

    for part, tile in enumerate(tiles):
        own_ref[part] = tile

    def copy(i, carry):
        for part, tile in enumerate(tiles):
            out_ref[i, part] = tile
        return carry

    lax.fori_loop(0, out_ref.shape[0], copy, 0)


def point_payload(ordering, coordinates, direction, copies):
    return pl.pallas_call(
        pick_points,
        out_shape=(
            jax.ShapeDtypeStruct((copies, 6, RHS, HALF), f32),
            jax.ShapeDtypeStruct((6, RHS, HALF), f32),
        ),
        in_specs=[
            pl.BlockSpec(memory_space=pltpu.HBM),
            pl.BlockSpec(memory_space=pltpu.HBM),
            pl.BlockSpec(memory_space=pltpu.VMEM),
        ],
        out_specs=(pl.BlockSpec(memory_space=pltpu.VMEM),) * 2,
        scratch_shapes=[
            pltpu.SMEM((PAIR,), jnp.int32),
            pltpu.VMEM(coordinates.shape, f32),
            pltpu.SemaphoreType.DMA((2,)),
        ],
        compiler_params=pltpu.CompilerParams(vmem_limit_bytes=56 * MEGA),
        name="pick_points",
    )(ordering, coordinates, direction)


TALL, WIDE = 512, 256


def image_kernel(pieces, own_ref, start_ref, *refs):
    columns, (out_ref, own_part, column_part, field_part, square) = refs[:pieces], refs[pieces:]
    each = pl.num_programs(0) // pieces

    @pl.when(pl.program_id(0) == 0)
    def _():
        for block in range(OWN):
            own_part[:, block * BS : (block + 1) * BS] = features(places(own_ref, block), True)
        out_ref[...] = start_ref[...]

    def prepare(columns_ref):
        for member in range(STEP):
            for block in range(OWN):
                at = OWN * member + block
                tiles = columns_ref.at[member]
                column_part[at * BS : (at + 1) * BS, :] = features(places(tiles, block), False).T
                field = jnp.concatenate([tiles[2 * block], tiles[2 * block + 1]], axis=1)
                field_part[at] = jnp.concatenate(split2(field * variance), axis=0)

    for index, columns_ref in enumerate(columns):
        pl.when(pl.program_id(0) // each == index)(functools.partial(prepare, columns_ref))
    jobs = [
        (q, r) for r in range(OWN * BS // WIDE) for q in range(STEP * OWN * BS // TALL)
    ]

    def fill(job, slot):
        q, r = jobs[job]
        square[slot] = jnp.dot(
            column_part[q * TALL : (q + 1) * TALL, :],
            own_part[:, r * WIDE : (r + 1) * WIDE],
            preferred_element_type=f32,
        )

    fill(0, 0)
    for job, (q, r) in enumerate(jobs):
        if job + 1 < len(jobs):
            fill(job + 1, (job + 1) % 2)
        for part in range(TALL // BS):
            for lanes in range(WIDE // HALF):
                x = square[
                    job % 2, part * BS : (part + 1) * BS, lanes * HALF : (lanes + 1) * HALF
                ]
                x = jnp.maximum(x, 1e-30)
                u = -offset - x * lax.rsqrt(x)
                tile = u * jnp.exp2(u)
                top, low = split2(tile)
                field = field_part[q * (TALL // BS) + part]
                where = slice(r * WIDE + lanes * HALF, r * WIDE + (lanes + 1) * HALF)
                out_ref[:, where] += jnp.dot(
                    field, top, preferred_element_type=f32
                ) + jnp.dot(field, low, preferred_element_type=f32)


def add_image(own, columns, start):
    pieces, count = len(columns), columns[0].shape[0]
    each = count // STEP
    pairs = pieces * count * OWN * BS * OWN * BS

    def piece_spec(index):
        return pl.BlockSpec(
            (STEP, 6, RHS, HALF),
            lambda i: (jnp.clip(i - index * each, 0, each - 1), 0, 0, 0),
        )

    return pl.pallas_call(
        functools.partial(image_kernel, pieces),
        grid=(pieces * each,),
        in_specs=[
            pl.BlockSpec((6, RHS, HALF), lambda i: (0, 0, 0)),
            pl.BlockSpec((2 * RHS, OWN * BS), lambda i: (0, 0)),
        ]
        + [piece_spec(index) for index in range(pieces)],
        out_specs=pl.BlockSpec((2 * RHS, OWN * BS), lambda i: (0, 0)),
        out_shape=jax.ShapeDtypeStruct((2 * RHS, OWN * BS), f32),
        scratch_shapes=[
            pltpu.VMEM((48, OWN * BS), bf16),
            pltpu.VMEM((STEP * OWN * BS, 48), bf16),
            pltpu.VMEM((OWN * STEP, 2 * RHS, BS), bf16),
            pltpu.VMEM((2, TALL, WIDE), f32),
        ],
        compiler_params=pltpu.CompilerParams(vmem_limit_bytes=10 * MEGA),
        cost_estimate=pl.CostEstimate(
            flops=600 * pairs, transcendentals=2 * pairs, bytes_accessed=pieces * count * 6 * 4096
        ),
        name="image",
    )(own, start, *columns)


def split_whitening(whitening_ref, whiten_top, whiten_low):
    rows = lax.broadcasted_iota(jnp.int32, (BS, BS), 0)
    lanes = lax.broadcasted_iota(jnp.int32, (BS, BS), 1)
    for b in range(OWN):
        whiten = whitening_ref[b] + jnp.where(rows == lanes, 1.0, 0.0)
        whiten_top[b], whiten_low[b] = split2(whiten)


def fetch_factors(far_cross, far_whitening, cross_ref, whitening_ref, sems):
    copies = [
        pltpu.make_async_copy(far_cross.at[b], cross_ref.at[b], sems.at[b]) for b in range(OWN)
    ]
    copies.insert(OWN, pltpu.make_async_copy(far_whitening, whitening_ref, sems.at[OWN]))
    for copy in copies:
        copy.start()
    return copies


def lower(near, valid_ref, cross_ref, field, block):
    total = field
    for k in range(NBR):
        at = block * NBR + k
        weight = valid_ref[at].astype(f32)
        total = total - pair_dot(near(at) * weight, *split2(cross_ref[block, k]), ((1,), (1,)))
    return total


def lanes_of(v):
    return v[:, :HALF] + v[:, HALF:]


def measure_kernel(
    list_ref, valid_ref, all_ref, residual_ref, far_cross, far_whitening, sum_ref, direction_ref,
    out_ref, near_ref, near_buf, whiten_top, whiten_low, cross_ref, whitening_ref, sems,
    factor_sems,
):
    factors = fetch_factors(far_cross, far_whitening, cross_ref, whitening_ref, factor_sems)
    copies = []
    for b in range(OWN):
        for k in range(NBR):
            at = b * NBR + k
            copies.append(
                pltpu.make_async_copy(all_ref.at[list_ref[at]], near_buf.at[at], sems.at[at])
            )
            copies[-1].start()
    for copy in copies:
        copy.wait()
    factors[OWN].wait()
    split_whitening(whitening_ref, whiten_top, whiten_low)
    old = jnp.zeros((RHS, HALF), f32)
    curvature = jnp.zeros((RHS, HALF), f32)
    tiles = []
    for b in range(OWN):
        factors[b].wait()
        lowered = lower(
            lambda at: near_buf[at], valid_ref, cross_ref, residual_ref[b], b
        )
        mapped = pair_dot(lowered, whiten_top[b], whiten_low[b], ((1,), (1,)))
        old = old + lanes_of(mapped * mapped)
        here = slice(b * BS, (b + 1) * BS)
        image = sum_ref[:RHS, here] + sum_ref[RHS:, here] + nugget * direction_ref[b]
        curvature = curvature + lanes_of(direction_ref[b] * image)
        tiles += [image[:, :HALF], image[:, HALF:]]
    lane = lax.broadcasted_iota(jnp.int32, (RHS, HALF), 1)
    old = jnp.sum(old, axis=1, keepdims=True)
    curvature = jnp.sum(curvature, axis=1, keepdims=True)
    tiles.append(jnp.where(lane == 0, old, jnp.where(lane == 1, curvature, 0.0)))

    def copy(i, carry):
        for part, tile in enumerate(tiles):
            out_ref[i, part] = tile
        return carry

    lax.fori_loop(0, out_ref.shape[0], copy, 0)
    near_ref[...] = near_buf[...]


def measure_step(lists, valid, gathered, residual, cross, whitening, total, direction):
    smem = pl.BlockSpec(memory_space=pltpu.SMEM)
    vmem = pl.BlockSpec(memory_space=pltpu.VMEM)
    far = pl.BlockSpec(memory_space=pl.ANY)
    return pl.pallas_call(
        measure_kernel,
        out_shape=(
            jax.ShapeDtypeStruct((PEERS, 5, RHS, HALF), f32),
            jax.ShapeDtypeStruct((OWN * NBR, RHS, BS), f32),
        ),
        in_specs=[smem, smem, far, vmem, far, far, vmem, vmem],
        out_specs=(vmem, vmem),
        scratch_shapes=[
            pltpu.VMEM((OWN * NBR, RHS, BS), f32),
            pltpu.VMEM((OWN, BS, BS), bf16),
            pltpu.VMEM((OWN, BS, BS), bf16),
            pltpu.VMEM((OWN, NBR, BS, BS), f32),
            pltpu.VMEM((OWN, BS, BS), f32),
            pltpu.SemaphoreType.DMA((OWN * NBR,)),
            pltpu.SemaphoreType.DMA((OWN + 1,)),
        ],
        compiler_params=pltpu.CompilerParams(vmem_limit_bytes=57 * MEGA),
        name="measure_step",
    )(lists, valid, gathered, residual, cross, whitening, total, direction)


def spread_kernel(
    at_ref, valid_ref, into_ref, self_ref, mine_ref, other_ref, near_ref, residual_ref, solution_ref,
    direction_ref, far_cross, far_whitening,
    solution_out, residual_out, scaled_out, out_ref, old_out,
    whiten_top, whiten_low, cross_ref, whitening_ref, factor_sems,
):
    factors = fetch_factors(far_cross, far_whitening, cross_ref, whitening_ref, factor_sems)
    total = jnp.zeros((RHS, HALF), f32)
    for i in range(PEERS):
        total = total + mine_ref[i, 4] + other_ref[i, 4]
    old = total[:, 0:1]
    step = old / total[:, 1:2]

    def clear(i, carry):
        for part in range(2 * OWN):
            out_ref[i, part] = jnp.zeros((RHS, HALF), f32)
        return carry

    lax.fori_loop(0, 2 * PEERS, clear, 0)

    def image_of(at):
        slot = at & 63
        a = jnp.concatenate([mine_ref[slot, 2 * (at >> 7)], mine_ref[slot, 2 * (at >> 7) + 1]], 1)
        b = jnp.concatenate([other_ref[slot, 2 * (at >> 7)], other_ref[slot, 2 * (at >> 7) + 1]], 1)
        return jnp.where(((at >> 6) & 1) == 0, a, b)

    newer = jnp.zeros((RHS, HALF), f32)
    factors[OWN].wait()
    split_whitening(whitening_ref, whiten_top, whiten_low)
    for b in range(OWN):
        factors[b].wait()
        solution_out[b] = solution_ref[b] + step * direction_ref[b]
        image = jnp.concatenate(
            [mine_ref[self_ref[0], 2 * b], mine_ref[self_ref[0], 2 * b + 1]], 1
        )
        following = residual_ref[b] - step * image
        residual_out[b] = following
        lowered = lower(
            lambda at: near_ref[at] - step * image_of(at_ref[at]),
            valid_ref, cross_ref, following, b,
        )
        mapped = pair_dot(lowered, whiten_top[b], whiten_low[b], ((1,), (1,)))
        newer = newer + lanes_of(mapped * mapped)
        scaled = pair_dot(mapped, whiten_top[b], whiten_low[b], ((1,), (0,)))
        scaled_out[b] = scaled
        for k in range(NBR):
            at = b * NBR + k
            spread = pair_dot(scaled, *split2(cross_ref[b, k]), ((1,), (0,)))
            spread = spread * valid_ref[at].astype(f32)
            to = into_ref[at]
            out_ref[to >> 1, 2 * (to & 1)] += spread[:, :HALF]
            out_ref[to >> 1, 2 * (to & 1) + 1] += spread[:, HALF:]
    newer = jnp.sum(newer, axis=1, keepdims=True)
    lane = lax.broadcasted_iota(jnp.int32, (RHS, HALF), 1)
    newer = jnp.where(lane == 0, newer, 0.0)

    def share(i, carry):
        out_ref[i, 2 * OWN] = newer
        return carry

    lax.fori_loop(0, 2 * PEERS, share, 0)
    old_out[...] = jnp.broadcast_to(old, (RHS, HALF))


def sum_kernel(all_ref, scaled_ref, direction_ref, old_ref, out_ref):
    total = all_ref[0]
    for i in range(1, PEERS):
        total = total + all_ref[i]
    ratio = total[2 * OWN, :, 0:1] / old_ref[:, 0:1]
    for b in range(OWN):
        back = jnp.concatenate([total[2 * b], total[2 * b + 1]], axis=1)
        out_ref[b] = scaled_ref[b] - back + ratio * direction_ref[b]


def sum_step(everything, scaled, direction, old):
    vmem = pl.BlockSpec(memory_space=pltpu.VMEM)
    return pl.pallas_call(
        sum_kernel,
        out_shape=jax.ShapeDtypeStruct((OWN, RHS, BS), f32),
        in_specs=[vmem] * 4,
        out_specs=vmem,
        compiler_params=pltpu.CompilerParams(vmem_limit_bytes=8 * MEGA),
        name="sum_step",
    )(everything, scaled, direction, old)


def spread_step(
    at, valid, into, self_at, mine, other, near, residual, solution, direction, cross, whitening
):
    smem = pl.BlockSpec(memory_space=pltpu.SMEM)
    vmem = pl.BlockSpec(memory_space=pltpu.VMEM)
    own = jax.ShapeDtypeStruct((OWN, RHS, BS), f32)
    return pl.pallas_call(
        spread_kernel,
        out_shape=(
            own,
            own,
            own,
            jax.ShapeDtypeStruct((2 * PEERS, 2 * OWN + 1, RHS, HALF), f32),
            jax.ShapeDtypeStruct((RHS, HALF), f32),
        ),
        in_specs=[smem] * 4 + [vmem] * 6 + [pl.BlockSpec(memory_space=pl.ANY)] * 2,
        out_specs=(vmem,) * 5,
        scratch_shapes=[
            pltpu.VMEM((OWN, BS, BS), bf16),
            pltpu.VMEM((OWN, BS, BS), bf16),
            pltpu.VMEM((OWN, NBR, BS, BS), f32),
            pltpu.VMEM((OWN, BS, BS), f32),
            pltpu.SemaphoreType.DMA((OWN + 1,)),
        ],
        compiler_params=pltpu.CompilerParams(vmem_limit_bytes=20 * MEGA),
        name="spread_step",
    )(
        at, valid, into, self_at, mine, other, near, residual, solution, direction, cross, whitening
    )


def x_around(hop):
    def target(i):
        return (i // 8 + hop) % 4 * 8 + i % 8

    return functools.partial(
        lax.ppermute, axis_name="col", perm=[(i, target(i)) for i in range(32)]
    )


def to_other_core(value):
    return lax.ppermute(value, "col", [(i, i ^ 1) for i in range(32)])


def exchange(value, groups):
    return lax.all_to_all(value, AXES, 0, 0, axis_index_groups=groups, tiled=True)


SAME_CORE = [[2 * j + core for j in range(PEERS)] for core in range(2)]
SAME_X_CORE = [
    [y * 32 + x * 8 + z * 2 + core for y in range(4) for z in range(4)]
    for x in range(4)
    for core in range(2)
]


def per_device(coordinates, ordering, neighbours, cross, whitening, solution, residual, direction):
    row = lax.axis_index("row")
    col = lax.axis_index("col")
    device = row * 32 + col
    here_core = device % 2
    own_ids = device * OWN + jnp.arange(OWN, dtype=jnp.int32)
    own_lists = lax.dynamic_slice_in_dim(neighbours, device * OWN, OWN, 0)
    valid = (own_lists < own_ids[:, None]).astype(jnp.int32).reshape(-1)
    lists = own_lists.reshape(-1)
    their = lists // OWN
    core_gap = (their % 2) ^ here_core
    at = ((lists % OWN) * 2 + core_gap) * PEERS + their // 2
    into = (core_gap * PEERS + their // 2) * OWN + lists % OWN
    self_at = (device // 2)[None]

    gathered = lax.all_gather(residual, AXES, axis=0, tiled=True)

    payload, own = point_payload(ordering, coordinates, direction, 16)
    plane = exchange(payload, SAME_X_CORE)
    plane, plane_other = lax.optimization_barrier((plane, to_other_core(plane)))
    beyond = [x_around(hop)(plane) for hop in (1, 3, 2)]
    total = add_image(own, [plane, plane_other], jnp.zeros((2 * RHS, OWN * BS), f32))
    others = [to_other_core(piece) for piece in beyond]
    total = add_image(own, beyond, total)
    total = add_image(own, others, total)

    image, near = measure_step(
        lists, valid, gathered, residual, cross, whitening, total, direction
    )
    mine = exchange(image, SAME_CORE)
    other = to_other_core(mine)
    solution_next, residual_next, scaled, back, old = spread_step(
        at, valid, into, self_at, mine, other, near, residual, solution, direction, cross, whitening
    )
    back = back[:PEERS] + to_other_core(back[PEERS:])
    direction_next = sum_step(exchange(back, SAME_CORE), scaled, direction, old)
    return (solution_next, residual_next, direction_next)


def solution(mesh):
    placed = (
        P(),
        P(),
        P(),
        P(("row", "col"), None, None, None),
        P(("row", "col"), None, None),
        P(("row", "col"), None, None),
        P(("row", "col"), None, None),
        P(("row", "col"), None, None),
    )
    return jax.shard_map(
        per_device,
        mesh=mesh,
        in_specs=placed,
        out_specs=(
            P(("row", "col"), None, None),
            P(("row", "col"), None, None),
            P(("row", "col"), None, None),
        ),
        check_vma=False,
    )
```

```python
import functools
import math

import jax
import jax.numpy as jnp
from jax import lax
from jax.experimental import pallas as pl
from jax.experimental.pallas import tpu as pltpu
from jax.sharding import PartitionSpec as P

f32 = jnp.float32
bf16 = jnp.bfloat16
rate = math.sqrt(3.0) / 0.3 * math.log2(math.e)
offset = 1.0 / math.log(2.0)
variance = -0.05 * math.e * math.log(2.0)
nugget = 1.0
AXES = ("row", "col")
BS, RHS, NBR, OWN = 256, 8, 4, 2
HALF = 128
STEP = 4
PEERS = 64
GUARD = 2.0**-20
PAIR = 2 * OWN * BS
MEGA = 1 << 20


def split2(v):
    top = v.astype(bf16)
    return top, (v - top.astype(f32)).astype(bf16)


def split3(v):
    top = v.astype(bf16).astype(f32)
    rest = v - top
    middle = rest.astype(bf16).astype(f32)
    return top, middle, rest - middle


def pair_dot(a, top, low, dims):
    both = jnp.concatenate(split2(a), axis=0)
    high = lax.dot_general(both, top, (dims, ((), ())), preferred_element_type=f32)
    rest = lax.dot_general(both, low, (dims, ((), ())), preferred_element_type=f32)
    return high[:RHS] + (high[RHS:] + (rest[:RHS] + rest[RHS:]))


def features(place, own):
    a = (place - 0.5) * rate
    norm = jnp.sum(a * a, axis=0, keepdims=True)
    one = jnp.ones_like(norm)
    pad = jnp.zeros((3, norm.shape[1]), f32)
    parts = [-2.0 * a, one, norm, pad] if own else [a, norm, one, pad]
    top, middle, low = split3(jnp.concatenate(parts, axis=0))
    order = [top, middle, top, middle, low, top] if own else [top, top, middle, middle, top, low]
    return jnp.concatenate(order, axis=0).astype(bf16)


def places(tiles, block):
    rows = slice(3 * block, 3 * block + 3)
    return jnp.concatenate([tiles[4, rows, :], tiles[5, rows, :]], axis=1)


def pick_points(
    all_order, all_coordinates, direction_ref, out_ref, own_ref, order_ref, coordinates_ref, sems
):
    device = lax.axis_index("row") * 32 + lax.axis_index("col")
    pair = pl.multiple_of(device // 2 * PAIR, PAIR)
    order_copy = pltpu.make_async_copy(all_order.at[pl.ds(pair, PAIR)], order_ref, sems.at[0])
    order_copy.start()
    copy_points = pltpu.make_async_copy(all_coordinates, coordinates_ref, sems.at[1])
    copy_points.start()
    order_copy.wait()
    copy_points.wait()
    first = device % 2 * (OWN * BS)
    lane = lax.broadcasted_iota(jnp.int32, (3, HALF), 1)
    groups = 2 * OWN

    def one_point(i, found):
        kept = []
        for group in range(groups):
            at = order_ref[first + group * HALF + i]
            base = pl.multiple_of((at >> 7) << 7, HALF)
            line = coordinates_ref[:, pl.ds(base, HALF)]
            turned = pltpu.roll(line, (i - (at & (HALF - 1))) & (HALF - 1), 1)
            kept.append(jnp.where(lane == i, turned, found[group]))
        return tuple(kept)

    found = lax.fori_loop(0, HALF, one_point, (jnp.zeros((3, HALF), f32),) * groups, unroll=16)
    pad = jnp.zeros((2, HALF), f32)
    tiles = []
    for block in range(OWN):
        for half in range(2):
            tiles.append(direction_ref[block, :, half * HALF : (half + 1) * HALF])
    for half in range(2):
        tiles.append(jnp.concatenate([found[half], found[2 + half], pad], axis=0))

    for part, tile in enumerate(tiles):
        own_ref[part] = tile

    def copy(i, carry):
        for part, tile in enumerate(tiles):
            out_ref[i, part] = tile
        return carry

    lax.fori_loop(0, out_ref.shape[0], copy, 0)


def point_payload(ordering, coordinates, direction, copies):
    return pl.pallas_call(
        pick_points,
        out_shape=(
            jax.ShapeDtypeStruct((copies, 6, RHS, HALF), f32),
            jax.ShapeDtypeStruct((6, RHS, HALF), f32),
        ),
        in_specs=[
            pl.BlockSpec(memory_space=pltpu.HBM),
            pl.BlockSpec(memory_space=pltpu.HBM),
            pl.BlockSpec(memory_space=pltpu.VMEM),
        ],
        out_specs=(pl.BlockSpec(memory_space=pltpu.VMEM),) * 2,
        scratch_shapes=[
            pltpu.SMEM((PAIR,), jnp.int32),
            pltpu.VMEM(coordinates.shape, f32),
            pltpu.SemaphoreType.DMA((2,)),
        ],
        compiler_params=pltpu.CompilerParams(vmem_limit_bytes=56 * MEGA),
        name="pick_points",
    )(ordering, coordinates, direction)


TALL, WIDE = 512, 256


def image_kernel(pieces, own_ref, start_ref, *refs):
    columns, (out_ref, own_part, column_part, field_part, square) = refs[:pieces], refs[pieces:]
    each = pl.num_programs(0) // pieces

    @pl.when(pl.program_id(0) == 0)
    def _():
        for block in range(OWN):
            own_part[:, block * BS : (block + 1) * BS] = features(places(own_ref, block), True)
        out_ref[...] = start_ref[...]

    def prepare(columns_ref):
        for member in range(STEP):
            for block in range(OWN):
                at = OWN * member + block
                tiles = columns_ref.at[member]
                column_part[at * BS : (at + 1) * BS, :] = features(places(tiles, block), False).T
                field = jnp.concatenate([tiles[2 * block], tiles[2 * block + 1]], axis=1)
                field_part[at] = jnp.concatenate(split2(field * variance), axis=0)

    for index, columns_ref in enumerate(columns):
        pl.when(pl.program_id(0) // each == index)(functools.partial(prepare, columns_ref))
    jobs = [
        (q, r) for r in range(OWN * BS // WIDE) for q in range(STEP * OWN * BS // TALL)
    ]

    def fill(job, slot):
        q, r = jobs[job]
        square[slot] = jnp.dot(
            column_part[q * TALL : (q + 1) * TALL, :],
            own_part[:, r * WIDE : (r + 1) * WIDE],
            preferred_element_type=f32,
        )

    fill(0, 0)
    for job, (q, r) in enumerate(jobs):
        if job + 1 < len(jobs):
            fill(job + 1, (job + 1) % 2)
        for part in range(TALL // BS):
            for lanes in range(WIDE // HALF):
                x = square[
                    job % 2, part * BS : (part + 1) * BS, lanes * HALF : (lanes + 1) * HALF
                ]
                u = -offset - x * lax.rsqrt(jnp.maximum(x, GUARD))
                tile = u * jnp.exp2(u)
                top, low = split2(tile)
                field = field_part[q * (TALL // BS) + part]
                where = slice(r * WIDE + lanes * HALF, r * WIDE + (lanes + 1) * HALF)
                out_ref[:, where] += jnp.dot(
                    field, top, preferred_element_type=f32
                ) + jnp.dot(field, low, preferred_element_type=f32)


def add_image(own, columns, start):
    pieces, count = len(columns), columns[0].shape[0]
    each = count // STEP
    pairs = pieces * count * OWN * BS * OWN * BS

    def piece_spec(index):
        return pl.BlockSpec(
            (STEP, 6, RHS, HALF),
            lambda i: (jnp.clip(i - index * each, 0, each - 1), 0, 0, 0),
        )

    return pl.pallas_call(
        functools.partial(image_kernel, pieces),
        grid=(pieces * each,),
        in_specs=[
            pl.BlockSpec((6, RHS, HALF), lambda i: (0, 0, 0)),
            pl.BlockSpec((2 * RHS, OWN * BS), lambda i: (0, 0)),
        ]
        + [piece_spec(index) for index in range(pieces)],
        out_specs=pl.BlockSpec((2 * RHS, OWN * BS), lambda i: (0, 0)),
        out_shape=jax.ShapeDtypeStruct((2 * RHS, OWN * BS), f32),
        scratch_shapes=[
            pltpu.VMEM((48, OWN * BS), bf16),
            pltpu.VMEM((STEP * OWN * BS, 48), bf16),
            pltpu.VMEM((OWN * STEP, 2 * RHS, BS), bf16),
            pltpu.VMEM((2, TALL, WIDE), f32),
        ],
        compiler_params=pltpu.CompilerParams(vmem_limit_bytes=10 * MEGA),
        cost_estimate=pl.CostEstimate(
            flops=600 * pairs, transcendentals=2 * pairs, bytes_accessed=pieces * count * 6 * 4096
        ),
        name="image",
    )(own, start, *columns)


def split_whitening(whitening_ref, whiten_top, whiten_low):
    rows = lax.broadcasted_iota(jnp.int32, (BS, BS), 0)
    lanes = lax.broadcasted_iota(jnp.int32, (BS, BS), 1)
    for b in range(OWN):
        whiten = whitening_ref[b] + jnp.where(rows == lanes, 1.0, 0.0)
        whiten_top[b], whiten_low[b] = split2(whiten)


def fetch_factors(far_cross, far_whitening, cross_ref, whitening_ref, sems):
    copies = [
        pltpu.make_async_copy(far_cross.at[b], cross_ref.at[b], sems.at[b]) for b in range(OWN)
    ]
    copies.insert(OWN, pltpu.make_async_copy(far_whitening, whitening_ref, sems.at[OWN]))
    for copy in copies:
        copy.start()
    return copies


def lower(near, valid_ref, cross_ref, field, block):
    total = field
    for k in range(NBR):
        at = block * NBR + k
        weight = valid_ref[at].astype(f32)
        total = total - pair_dot(near(at) * weight, *split2(cross_ref[block, k]), ((1,), (1,)))
    return total


def lanes_of(v):
    return v[:, :HALF] + v[:, HALF:]


def measure_kernel(
    list_ref, valid_ref, all_ref, residual_ref, far_cross, far_whitening, sum_ref, direction_ref,
    out_ref, near_ref, near_buf, whiten_top, whiten_low, cross_ref, whitening_ref, sems,
    factor_sems,
):
    factors = fetch_factors(far_cross, far_whitening, cross_ref, whitening_ref, factor_sems)
    copies = []
    for b in range(OWN):
        for k in range(NBR):
            at = b * NBR + k
            copies.append(
                pltpu.make_async_copy(all_ref.at[list_ref[at]], near_buf.at[at], sems.at[at])
            )
            copies[-1].start()
    for copy in copies:
        copy.wait()
    factors[OWN].wait()
    split_whitening(whitening_ref, whiten_top, whiten_low)
    old = jnp.zeros((RHS, HALF), f32)
    curvature = jnp.zeros((RHS, HALF), f32)
    tiles = []
    for b in range(OWN):
        factors[b].wait()
        lowered = lower(
            lambda at: near_buf[at], valid_ref, cross_ref, residual_ref[b], b
        )
        mapped = pair_dot(lowered, whiten_top[b], whiten_low[b], ((1,), (1,)))
        old = old + lanes_of(mapped * mapped)
        here = slice(b * BS, (b + 1) * BS)
        image = sum_ref[:RHS, here] + sum_ref[RHS:, here] + nugget * direction_ref[b]
        curvature = curvature + lanes_of(direction_ref[b] * image)
        tiles += [image[:, :HALF], image[:, HALF:]]
    lane = lax.broadcasted_iota(jnp.int32, (RHS, HALF), 1)
    old = jnp.sum(old, axis=1, keepdims=True)
    curvature = jnp.sum(curvature, axis=1, keepdims=True)
    tiles.append(jnp.where(lane == 0, old, jnp.where(lane == 1, curvature, 0.0)))

    def copy(i, carry):
        for part, tile in enumerate(tiles):
            out_ref[i, part] = tile
        return carry

    lax.fori_loop(0, out_ref.shape[0], copy, 0)
    near_ref[...] = near_buf[...]


def measure_step(lists, valid, gathered, residual, cross, whitening, total, direction):
    smem = pl.BlockSpec(memory_space=pltpu.SMEM)
    vmem = pl.BlockSpec(memory_space=pltpu.VMEM)
    far = pl.BlockSpec(memory_space=pl.ANY)
    return pl.pallas_call(
        measure_kernel,
        out_shape=(
            jax.ShapeDtypeStruct((PEERS, 5, RHS, HALF), f32),
            jax.ShapeDtypeStruct((OWN * NBR, RHS, BS), f32),
        ),
        in_specs=[smem, smem, far, vmem, far, far, vmem, vmem],
        out_specs=(vmem, vmem),
        scratch_shapes=[
            pltpu.VMEM((OWN * NBR, RHS, BS), f32),
            pltpu.VMEM((OWN, BS, BS), bf16),
            pltpu.VMEM((OWN, BS, BS), bf16),
            pltpu.VMEM((OWN, NBR, BS, BS), f32),
            pltpu.VMEM((OWN, BS, BS), f32),
            pltpu.SemaphoreType.DMA((OWN * NBR,)),
            pltpu.SemaphoreType.DMA((OWN + 1,)),
        ],
        compiler_params=pltpu.CompilerParams(vmem_limit_bytes=12 * MEGA),
        name="measure_step",
    )(lists, valid, gathered, residual, cross, whitening, total, direction)


def spread_kernel(
    at_ref, valid_ref, into_ref, self_ref, mine_ref, other_ref, near_ref, residual_ref, solution_ref,
    direction_ref, far_cross, far_whitening,
    solution_out, residual_out, scaled_out, out_ref, old_out,
    whiten_top, whiten_low, cross_ref, whitening_ref, factor_sems,
):
    factors = fetch_factors(far_cross, far_whitening, cross_ref, whitening_ref, factor_sems)
    total = jnp.zeros((RHS, HALF), f32)
    for i in range(PEERS):
        total = total + mine_ref[i, 4] + other_ref[i, 4]
    old = total[:, 0:1]
    step = old / total[:, 1:2]

    def clear(i, carry):
        for part in range(2 * OWN):
            out_ref[i, part] = jnp.zeros((RHS, HALF), f32)
        return carry

    lax.fori_loop(0, 2 * PEERS, clear, 0)

    def image_of(at):
        slot = at & 63
        a = jnp.concatenate([mine_ref[slot, 2 * (at >> 7)], mine_ref[slot, 2 * (at >> 7) + 1]], 1)
        b = jnp.concatenate([other_ref[slot, 2 * (at >> 7)], other_ref[slot, 2 * (at >> 7) + 1]], 1)
        return jnp.where(((at >> 6) & 1) == 0, a, b)

    newer = jnp.zeros((RHS, HALF), f32)
    factors[OWN].wait()
    split_whitening(whitening_ref, whiten_top, whiten_low)
    for b in range(OWN):
        factors[b].wait()
        solution_out[b] = solution_ref[b] + step * direction_ref[b]
        image = jnp.concatenate(
            [mine_ref[self_ref[0], 2 * b], mine_ref[self_ref[0], 2 * b + 1]], 1
        )
        following = residual_ref[b] - step * image
        residual_out[b] = following
        lowered = lower(
            lambda at: near_ref[at] - step * image_of(at_ref[at]),
            valid_ref, cross_ref, following, b,
        )
        mapped = pair_dot(lowered, whiten_top[b], whiten_low[b], ((1,), (1,)))
        newer = newer + lanes_of(mapped * mapped)
        scaled = pair_dot(mapped, whiten_top[b], whiten_low[b], ((1,), (0,)))
        scaled_out[b] = scaled
        for k in range(NBR):
            at = b * NBR + k
            spread = pair_dot(scaled, *split2(cross_ref[b, k]), ((1,), (0,)))
            spread = spread * valid_ref[at].astype(f32)
            to = into_ref[at]
            out_ref[to >> 1, 2 * (to & 1)] += spread[:, :HALF]
            out_ref[to >> 1, 2 * (to & 1) + 1] += spread[:, HALF:]
    newer = jnp.sum(newer, axis=1, keepdims=True)
    lane = lax.broadcasted_iota(jnp.int32, (RHS, HALF), 1)
    newer = jnp.where(lane == 0, newer, 0.0)

    def share(i, carry):
        out_ref[i, 2 * OWN] = newer
        return carry

    lax.fori_loop(0, 2 * PEERS, share, 0)
    old_out[...] = jnp.broadcast_to(old, (RHS, HALF))


def sum_kernel(all_ref, scaled_ref, direction_ref, old_ref, out_ref):
    total = all_ref[0]
    for i in range(1, PEERS):
        total = total + all_ref[i]
    ratio = total[2 * OWN, :, 0:1] / old_ref[:, 0:1]
    for b in range(OWN):
        back = jnp.concatenate([total[2 * b], total[2 * b + 1]], axis=1)
        out_ref[b] = scaled_ref[b] - back + ratio * direction_ref[b]


def sum_step(everything, scaled, direction, old):
    vmem = pl.BlockSpec(memory_space=pltpu.VMEM)
    return pl.pallas_call(
        sum_kernel,
        out_shape=jax.ShapeDtypeStruct((OWN, RHS, BS), f32),
        in_specs=[vmem] * 4,
        out_specs=vmem,
        compiler_params=pltpu.CompilerParams(vmem_limit_bytes=8 * MEGA),
        name="sum_step",
    )(everything, scaled, direction, old)


def spread_step(
    at, valid, into, self_at, mine, other, near, residual, solution, direction, cross, whitening
):
    smem = pl.BlockSpec(memory_space=pltpu.SMEM)
    vmem = pl.BlockSpec(memory_space=pltpu.VMEM)
    own = jax.ShapeDtypeStruct((OWN, RHS, BS), f32)
    return pl.pallas_call(
        spread_kernel,
        out_shape=(
            own,
            own,
            own,
            jax.ShapeDtypeStruct((2 * PEERS, 2 * OWN + 1, RHS, HALF), f32),
            jax.ShapeDtypeStruct((RHS, HALF), f32),
        ),
        in_specs=[smem] * 4 + [vmem] * 6 + [pl.BlockSpec(memory_space=pl.ANY)] * 2,
        out_specs=(vmem,) * 5,
        scratch_shapes=[
            pltpu.VMEM((OWN, BS, BS), bf16),
            pltpu.VMEM((OWN, BS, BS), bf16),
            pltpu.VMEM((OWN, NBR, BS, BS), f32),
            pltpu.VMEM((OWN, BS, BS), f32),
            pltpu.SemaphoreType.DMA((OWN + 1,)),
        ],
        compiler_params=pltpu.CompilerParams(vmem_limit_bytes=20 * MEGA),
        name="spread_step",
    )(
        at, valid, into, self_at, mine, other, near, residual, solution, direction, cross, whitening
    )


def x_around(hop):
    def target(i):
        return (i // 8 + hop) % 4 * 8 + i % 8

    return functools.partial(
        lax.ppermute, axis_name="col", perm=[(i, target(i)) for i in range(32)]
    )


def to_other_core(value):
    return lax.ppermute(value, "col", [(i, i ^ 1) for i in range(32)])


def exchange(value, groups):
    return lax.all_to_all(value, AXES, 0, 0, axis_index_groups=groups, tiled=True)


SAME_CORE = [[2 * j + core for j in range(PEERS)] for core in range(2)]
SAME_X_CORE = [
    [y * 32 + x * 8 + z * 2 + core for y in range(4) for z in range(4)]
    for x in range(4)
    for core in range(2)
]


def per_device(coordinates, ordering, neighbours, cross, whitening, solution, residual, direction):
    row = lax.axis_index("row")
    col = lax.axis_index("col")
    device = row * 32 + col
    here_core = device % 2
    own_ids = device * OWN + jnp.arange(OWN, dtype=jnp.int32)
    own_lists = lax.dynamic_slice_in_dim(neighbours, device * OWN, OWN, 0)
    valid = (own_lists < own_ids[:, None]).astype(jnp.int32).reshape(-1)
    lists = own_lists.reshape(-1)
    their = lists // OWN
    core_gap = (their % 2) ^ here_core
    at = ((lists % OWN) * 2 + core_gap) * PEERS + their // 2
    into = (core_gap * PEERS + their // 2) * OWN + lists % OWN
    self_at = (device // 2)[None]

    gathered = lax.all_gather(residual, AXES, axis=0, tiled=True)

    payload, own = point_payload(ordering, coordinates, direction, 16)
    plane = exchange(payload, SAME_X_CORE)
    plane, plane_other = lax.optimization_barrier((plane, to_other_core(plane)))
    beyond = [x_around(hop)(plane) for hop in (1, 3, 2)]
    total = add_image(own, [plane, plane_other], jnp.zeros((2 * RHS, OWN * BS), f32))
    others = [to_other_core(piece) for piece in beyond]
    total = add_image(own, beyond, total)
    total = add_image(own, others, total)

    image, near = measure_step(
        lists, valid, gathered, residual, cross, whitening, total, direction
    )
    mine = exchange(image, SAME_CORE)
    other = to_other_core(mine)
    solution_next, residual_next, scaled, back, old = spread_step(
        at, valid, into, self_at, mine, other, near, residual, solution, direction, cross, whitening
    )
    back = back[:PEERS] + to_other_core(back[PEERS:])
    direction_next = sum_step(exchange(back, SAME_CORE), scaled, direction, old)
    return (solution_next, residual_next, direction_next)


def solution(mesh):
    placed = (
        P(),
        P(),
        P(),
        P(("row", "col"), None, None, None),
        P(("row", "col"), None, None),
        P(("row", "col"), None, None),
        P(("row", "col"), None, None),
        P(("row", "col"), None, None),
    )
    return jax.shard_map(
        per_device,
        mesh=mesh,
        in_specs=placed,
        out_specs=(
            P(("row", "col"), None, None),
            P(("row", "col"), None, None),
            P(("row", "col"), None, None),
        ),
        check_vma=False,
    )
```

```python
import functools
import math

import jax
import jax.numpy as jnp
from jax import lax
from jax.experimental import pallas as pl
from jax.experimental.pallas import tpu as pltpu
from jax.sharding import PartitionSpec as P

f32 = jnp.float32
bf16 = jnp.bfloat16
rate = math.sqrt(3.0) / 0.3 * math.log2(math.e)
offset = 1.0 / math.log(2.0)
variance = -0.05 * math.e * math.log(2.0)
nugget = 1.0
AXES = ("row", "col")
BS, RHS, NBR, OWN = 256, 8, 4, 2
HALF = 128
STEP = 8
PEERS = 64
GUARD = 2.0**-20
PAIR = 2 * OWN * BS
MEGA = 1 << 20


def split2(v):
    top = v.astype(bf16)
    return top, (v - top.astype(f32)).astype(bf16)


def split3(v):
    top = v.astype(bf16).astype(f32)
    rest = v - top
    middle = rest.astype(bf16).astype(f32)
    return top, middle, rest - middle


def pair_dot(a, top, low, dims):
    both = jnp.concatenate(split2(a), axis=0)
    high = lax.dot_general(both, top, (dims, ((), ())), preferred_element_type=f32)
    rest = lax.dot_general(both, low, (dims, ((), ())), preferred_element_type=f32)
    return high[:RHS] + (high[RHS:] + (rest[:RHS] + rest[RHS:]))


def features(place, own):
    a = (place - 0.5) * rate
    norm = jnp.sum(a * a, axis=0, keepdims=True)
    one = jnp.ones_like(norm)
    pad = jnp.zeros((3, norm.shape[1]), f32)
    parts = [-2.0 * a, one, norm, pad] if own else [a, norm, one, pad]
    top, middle, low = split3(jnp.concatenate(parts, axis=0))
    order = [top, middle, top, middle, low, top] if own else [top, top, middle, middle, top, low]
    return jnp.concatenate(order, axis=0).astype(bf16)


def places(tiles, block):
    rows = slice(3 * block, 3 * block + 3)
    return jnp.concatenate([tiles[4, rows, :], tiles[5, rows, :]], axis=1)


def pick_points(
    all_order, all_coordinates, direction_ref, out_ref, own_ref, order_ref, coordinates_ref, sems
):
    device = lax.axis_index("row") * 32 + lax.axis_index("col")
    pair = pl.multiple_of(device // 2 * PAIR, PAIR)
    order_copy = pltpu.make_async_copy(all_order.at[pl.ds(pair, PAIR)], order_ref, sems.at[0])
    order_copy.start()
    copy_points = pltpu.make_async_copy(all_coordinates, coordinates_ref, sems.at[1])
    copy_points.start()
    order_copy.wait()
    copy_points.wait()
    first = device % 2 * (OWN * BS)
    lane = lax.broadcasted_iota(jnp.int32, (3, HALF), 1)
    groups = 2 * OWN

    def one_point(i, found):
        kept = []
        for group in range(groups):
            at = order_ref[first + group * HALF + i]
            base = pl.multiple_of((at >> 7) << 7, HALF)
            line = coordinates_ref[:, pl.ds(base, HALF)]
            turned = pltpu.roll(line, (i - (at & (HALF - 1))) & (HALF - 1), 1)
            kept.append(jnp.where(lane == i, turned, found[group]))
        return tuple(kept)

    found = lax.fori_loop(0, HALF, one_point, (jnp.zeros((3, HALF), f32),) * groups, unroll=16)
    pad = jnp.zeros((2, HALF), f32)
    tiles = []
    for block in range(OWN):
        for half in range(2):
            tiles.append(direction_ref[block, :, half * HALF : (half + 1) * HALF])
    for half in range(2):
        tiles.append(jnp.concatenate([found[half], found[2 + half], pad], axis=0))

    for part, tile in enumerate(tiles):
        own_ref[part] = tile

    def copy(i, carry):
        for part, tile in enumerate(tiles):
            out_ref[i, part] = tile
        return carry

    lax.fori_loop(0, out_ref.shape[0], copy, 0)


def point_payload(ordering, coordinates, direction, copies):
    return pl.pallas_call(
        pick_points,
        out_shape=(
            jax.ShapeDtypeStruct((copies, 6, RHS, HALF), f32),
            jax.ShapeDtypeStruct((6, RHS, HALF), f32),
        ),
        in_specs=[
            pl.BlockSpec(memory_space=pltpu.HBM),
            pl.BlockSpec(memory_space=pltpu.HBM),
            pl.BlockSpec(memory_space=pltpu.VMEM),
        ],
        out_specs=(pl.BlockSpec(memory_space=pltpu.VMEM),) * 2,
        scratch_shapes=[
            pltpu.SMEM((PAIR,), jnp.int32),
            pltpu.VMEM(coordinates.shape, f32),
            pltpu.SemaphoreType.DMA((2,)),
        ],
        compiler_params=pltpu.CompilerParams(vmem_limit_bytes=56 * MEGA),
        name="pick_points",
    )(ordering, coordinates, direction)


TALL, WIDE = 512, 256


def image_kernel(pieces, own_ref, start_ref, *refs):
    columns, (out_ref, own_part, column_part, field_part, square) = refs[:pieces], refs[pieces:]
    each = pl.num_programs(0) // pieces

    @pl.when(pl.program_id(0) == 0)
    def _():
        for block in range(OWN):
            own_part[:, block * BS : (block + 1) * BS] = features(places(own_ref, block), True)
        out_ref[...] = start_ref[...]

    def prepare(columns_ref):
        for member in range(STEP):
            for block in range(OWN):
                at = OWN * member + block
                tiles = columns_ref.at[member]
                column_part[at * BS : (at + 1) * BS, :] = features(places(tiles, block), False).T
                field = jnp.concatenate([tiles[2 * block], tiles[2 * block + 1]], axis=1)
                field_part[at] = jnp.concatenate(split2(field * variance), axis=0)

    for index, columns_ref in enumerate(columns):
        pl.when(pl.program_id(0) // each == index)(functools.partial(prepare, columns_ref))
    jobs = [
        (q, r) for r in range(OWN * BS // WIDE) for q in range(STEP * OWN * BS // TALL)
    ]

    def fill(job, slot):
        q, r = jobs[job]
        square[slot] = jnp.dot(
            column_part[q * TALL : (q + 1) * TALL, :],
            own_part[:, r * WIDE : (r + 1) * WIDE],
            preferred_element_type=f32,
        )

    fill(0, 0)
    for job, (q, r) in enumerate(jobs):
        if job + 1 < len(jobs):
            fill(job + 1, (job + 1) % 2)
        for part in range(TALL // BS):
            for lanes in range(WIDE // HALF):
                x = square[
                    job % 2, part * BS : (part + 1) * BS, lanes * HALF : (lanes + 1) * HALF
                ]
                u = -offset - x * lax.rsqrt(jnp.maximum(x, GUARD))
                tile = u * jnp.exp2(u)
                top, low = split2(tile)
                field = field_part[q * (TALL // BS) + part]
                where = slice(r * WIDE + lanes * HALF, r * WIDE + (lanes + 1) * HALF)
                out_ref[:, where] += jnp.dot(
                    field, top, preferred_element_type=f32
                ) + jnp.dot(field, low, preferred_element_type=f32)


def add_image(own, columns, start):
    pieces, count = len(columns), columns[0].shape[0]
    each = count // STEP
    pairs = pieces * count * OWN * BS * OWN * BS

    def piece_spec(index):
        return pl.BlockSpec(
            (STEP, 6, RHS, HALF),
            lambda i: (jnp.clip(i - index * each, 0, each - 1), 0, 0, 0),
        )

    return pl.pallas_call(
        functools.partial(image_kernel, pieces),
        grid=(pieces * each,),
        in_specs=[
            pl.BlockSpec((6, RHS, HALF), lambda i: (0, 0, 0)),
            pl.BlockSpec((2 * RHS, OWN * BS), lambda i: (0, 0)),
        ]
        + [piece_spec(index) for index in range(pieces)],
        out_specs=pl.BlockSpec((2 * RHS, OWN * BS), lambda i: (0, 0)),
        out_shape=jax.ShapeDtypeStruct((2 * RHS, OWN * BS), f32),
        scratch_shapes=[
            pltpu.VMEM((48, OWN * BS), bf16),
            pltpu.VMEM((STEP * OWN * BS, 48), bf16),
            pltpu.VMEM((OWN * STEP, 2 * RHS, BS), bf16),
            pltpu.VMEM((2, TALL, WIDE), f32),
        ],
        compiler_params=pltpu.CompilerParams(vmem_limit_bytes=10 * MEGA),
        cost_estimate=pl.CostEstimate(
            flops=600 * pairs, transcendentals=2 * pairs, bytes_accessed=pieces * count * 6 * 4096
        ),
        name="image",
    )(own, start, *columns)


def split_whitening(whitening_ref, whiten_top, whiten_low):
    rows = lax.broadcasted_iota(jnp.int32, (BS, BS), 0)
    lanes = lax.broadcasted_iota(jnp.int32, (BS, BS), 1)
    for b in range(OWN):
        whiten = whitening_ref[b] + jnp.where(rows == lanes, 1.0, 0.0)
        whiten_top[b], whiten_low[b] = split2(whiten)


def fetch_factors(far_cross, far_whitening, cross_ref, whitening_ref, sems):
    copies = [
        pltpu.make_async_copy(far_cross.at[b], cross_ref.at[b], sems.at[b]) for b in range(OWN)
    ]
    copies.insert(OWN, pltpu.make_async_copy(far_whitening, whitening_ref, sems.at[OWN]))
    for copy in copies:
        copy.start()
    return copies


def lower(near, valid_ref, cross_ref, field, block):
    total = field
    for k in range(NBR):
        at = block * NBR + k
        weight = valid_ref[at].astype(f32)
        total = total - pair_dot(near(at) * weight, *split2(cross_ref[block, k]), ((1,), (1,)))
    return total


def lanes_of(v):
    return v[:, :HALF] + v[:, HALF:]


def measure_kernel(
    list_ref, valid_ref, all_ref, residual_ref, far_cross, far_whitening, sum_ref, direction_ref,
    out_ref, near_ref, near_buf, whiten_top, whiten_low, cross_ref, whitening_ref, sems,
    factor_sems,
):
    factors = fetch_factors(far_cross, far_whitening, cross_ref, whitening_ref, factor_sems)
    copies = []
    for b in range(OWN):
        for k in range(NBR):
            at = b * NBR + k
            copies.append(
                pltpu.make_async_copy(all_ref.at[list_ref[at]], near_buf.at[at], sems.at[at])
            )
            copies[-1].start()
    for copy in copies:
        copy.wait()
    factors[OWN].wait()
    split_whitening(whitening_ref, whiten_top, whiten_low)
    old = jnp.zeros((RHS, HALF), f32)
    curvature = jnp.zeros((RHS, HALF), f32)
    tiles = []
    for b in range(OWN):
        factors[b].wait()
        lowered = lower(
            lambda at: near_buf[at], valid_ref, cross_ref, residual_ref[b], b
        )
        mapped = pair_dot(lowered, whiten_top[b], whiten_low[b], ((1,), (1,)))
        old = old + lanes_of(mapped * mapped)
        here = slice(b * BS, (b + 1) * BS)
        image = sum_ref[:RHS, here] + sum_ref[RHS:, here] + nugget * direction_ref[b]
        curvature = curvature + lanes_of(direction_ref[b] * image)
        tiles += [image[:, :HALF], image[:, HALF:]]
    lane = lax.broadcasted_iota(jnp.int32, (RHS, HALF), 1)
    old = jnp.sum(old, axis=1, keepdims=True)
    curvature = jnp.sum(curvature, axis=1, keepdims=True)
    tiles.append(jnp.where(lane == 0, old, jnp.where(lane == 1, curvature, 0.0)))

    def copy(i, carry):
        for part, tile in enumerate(tiles):
            out_ref[i, part] = tile
        return carry

    lax.fori_loop(0, out_ref.shape[0], copy, 0)
    near_ref[...] = near_buf[...]


def measure_step(lists, valid, gathered, residual, cross, whitening, total, direction):
    smem = pl.BlockSpec(memory_space=pltpu.SMEM)
    vmem = pl.BlockSpec(memory_space=pltpu.VMEM)
    far = pl.BlockSpec(memory_space=pl.ANY)
    return pl.pallas_call(
        measure_kernel,
        out_shape=(
            jax.ShapeDtypeStruct((PEERS, 5, RHS, HALF), f32),
            jax.ShapeDtypeStruct((OWN * NBR, RHS, BS), f32),
        ),
        in_specs=[smem, smem, far, vmem, far, far, vmem, vmem],
        out_specs=(vmem, vmem),
        scratch_shapes=[
            pltpu.VMEM((OWN * NBR, RHS, BS), f32),
            pltpu.VMEM((OWN, BS, BS), bf16),
            pltpu.VMEM((OWN, BS, BS), bf16),
            pltpu.VMEM((OWN, NBR, BS, BS), f32),
            pltpu.VMEM((OWN, BS, BS), f32),
            pltpu.SemaphoreType.DMA((OWN * NBR,)),
            pltpu.SemaphoreType.DMA((OWN + 1,)),
        ],
        compiler_params=pltpu.CompilerParams(vmem_limit_bytes=12 * MEGA),
        name="measure_step",
    )(lists, valid, gathered, residual, cross, whitening, total, direction)


def spread_kernel(
    at_ref, valid_ref, into_ref, self_ref, mine_ref, other_ref, near_ref, residual_ref, solution_ref,
    direction_ref, far_cross, far_whitening,
    solution_out, residual_out, scaled_out, out_ref, old_out,
    whiten_top, whiten_low, cross_ref, whitening_ref, factor_sems,
):
    factors = fetch_factors(far_cross, far_whitening, cross_ref, whitening_ref, factor_sems)
    total = jnp.zeros((RHS, HALF), f32)
    for i in range(PEERS):
        total = total + mine_ref[i, 4] + other_ref[i, 4]
    old = total[:, 0:1]
    step = old / total[:, 1:2]

    def clear(i, carry):
        for part in range(2 * OWN):
            out_ref[i, part] = jnp.zeros((RHS, HALF), f32)
        return carry

    lax.fori_loop(0, 2 * PEERS, clear, 0)

    def image_of(at):
        slot = at & 63
        a = jnp.concatenate([mine_ref[slot, 2 * (at >> 7)], mine_ref[slot, 2 * (at >> 7) + 1]], 1)
        b = jnp.concatenate([other_ref[slot, 2 * (at >> 7)], other_ref[slot, 2 * (at >> 7) + 1]], 1)
        return jnp.where(((at >> 6) & 1) == 0, a, b)

    newer = jnp.zeros((RHS, HALF), f32)
    factors[OWN].wait()
    split_whitening(whitening_ref, whiten_top, whiten_low)
    for b in range(OWN):
        factors[b].wait()
        solution_out[b] = solution_ref[b] + step * direction_ref[b]
        image = jnp.concatenate(
            [mine_ref[self_ref[0], 2 * b], mine_ref[self_ref[0], 2 * b + 1]], 1
        )
        following = residual_ref[b] - step * image
        residual_out[b] = following
        lowered = lower(
            lambda at: near_ref[at] - step * image_of(at_ref[at]),
            valid_ref, cross_ref, following, b,
        )
        mapped = pair_dot(lowered, whiten_top[b], whiten_low[b], ((1,), (1,)))
        newer = newer + lanes_of(mapped * mapped)
        scaled = pair_dot(mapped, whiten_top[b], whiten_low[b], ((1,), (0,)))
        scaled_out[b] = scaled
        for k in range(NBR):
            at = b * NBR + k
            spread = pair_dot(scaled, *split2(cross_ref[b, k]), ((1,), (0,)))
            spread = spread * valid_ref[at].astype(f32)
            to = into_ref[at]
            out_ref[to >> 1, 2 * (to & 1)] += spread[:, :HALF]
            out_ref[to >> 1, 2 * (to & 1) + 1] += spread[:, HALF:]
    newer = jnp.sum(newer, axis=1, keepdims=True)
    lane = lax.broadcasted_iota(jnp.int32, (RHS, HALF), 1)
    newer = jnp.where(lane == 0, newer, 0.0)

    def share(i, carry):
        out_ref[i, 2 * OWN] = newer
        return carry

    lax.fori_loop(0, 2 * PEERS, share, 0)
    old_out[...] = jnp.broadcast_to(old, (RHS, HALF))


def sum_kernel(all_ref, scaled_ref, direction_ref, old_ref, out_ref):
    total = all_ref[0]
    for i in range(1, PEERS):
        total = total + all_ref[i]
    ratio = total[2 * OWN, :, 0:1] / old_ref[:, 0:1]
    for b in range(OWN):
        back = jnp.concatenate([total[2 * b], total[2 * b + 1]], axis=1)
        out_ref[b] = scaled_ref[b] - back + ratio * direction_ref[b]


def sum_step(everything, scaled, direction, old):
    vmem = pl.BlockSpec(memory_space=pltpu.VMEM)
    return pl.pallas_call(
        sum_kernel,
        out_shape=jax.ShapeDtypeStruct((OWN, RHS, BS), f32),
        in_specs=[vmem] * 4,
        out_specs=vmem,
        compiler_params=pltpu.CompilerParams(vmem_limit_bytes=8 * MEGA),
        name="sum_step",
    )(everything, scaled, direction, old)


def spread_step(
    at, valid, into, self_at, mine, other, near, residual, solution, direction, cross, whitening
):
    smem = pl.BlockSpec(memory_space=pltpu.SMEM)
    vmem = pl.BlockSpec(memory_space=pltpu.VMEM)
    own = jax.ShapeDtypeStruct((OWN, RHS, BS), f32)
    return pl.pallas_call(
        spread_kernel,
        out_shape=(
            own,
            own,
            own,
            jax.ShapeDtypeStruct((2 * PEERS, 2 * OWN + 1, RHS, HALF), f32),
            jax.ShapeDtypeStruct((RHS, HALF), f32),
        ),
        in_specs=[smem] * 4 + [vmem] * 6 + [pl.BlockSpec(memory_space=pl.ANY)] * 2,
        out_specs=(vmem,) * 5,
        scratch_shapes=[
            pltpu.VMEM((OWN, BS, BS), bf16),
            pltpu.VMEM((OWN, BS, BS), bf16),
            pltpu.VMEM((OWN, NBR, BS, BS), f32),
            pltpu.VMEM((OWN, BS, BS), f32),
            pltpu.SemaphoreType.DMA((OWN + 1,)),
        ],
        compiler_params=pltpu.CompilerParams(vmem_limit_bytes=20 * MEGA),
        name="spread_step",
    )(
        at, valid, into, self_at, mine, other, near, residual, solution, direction, cross, whitening
    )


def x_around(hop):
    def target(i):
        return (i // 8 + hop) % 4 * 8 + i % 8

    return functools.partial(
        lax.ppermute, axis_name="col", perm=[(i, target(i)) for i in range(32)]
    )


def to_other_core(value):
    return lax.ppermute(value, "col", [(i, i ^ 1) for i in range(32)])


def exchange(value, groups):
    return lax.all_to_all(value, AXES, 0, 0, axis_index_groups=groups, tiled=True)


SAME_CORE = [[2 * j + core for j in range(PEERS)] for core in range(2)]
SAME_X_CORE = [
    [y * 32 + x * 8 + z * 2 + core for y in range(4) for z in range(4)]
    for x in range(4)
    for core in range(2)
]


def per_device(coordinates, ordering, neighbours, cross, whitening, solution, residual, direction):
    row = lax.axis_index("row")
    col = lax.axis_index("col")
    device = row * 32 + col
    here_core = device % 2
    own_ids = device * OWN + jnp.arange(OWN, dtype=jnp.int32)
    own_lists = lax.dynamic_slice_in_dim(neighbours, device * OWN, OWN, 0)
    valid = (own_lists < own_ids[:, None]).astype(jnp.int32).reshape(-1)
    lists = own_lists.reshape(-1)
    their = lists // OWN
    core_gap = (their % 2) ^ here_core
    at = ((lists % OWN) * 2 + core_gap) * PEERS + their // 2
    into = (core_gap * PEERS + their // 2) * OWN + lists % OWN
    self_at = (device // 2)[None]

    gathered = lax.all_gather(residual, AXES, axis=0, tiled=True)

    payload, own = point_payload(ordering, coordinates, direction, 16)
    plane = exchange(payload, SAME_X_CORE)
    plane, plane_other = lax.optimization_barrier((plane, to_other_core(plane)))
    beyond = [x_around(hop)(plane) for hop in (1, 3, 2)]
    total = add_image(own, [plane, plane_other], jnp.zeros((2 * RHS, OWN * BS), f32))
    others = [to_other_core(piece) for piece in beyond]
    total = add_image(own, beyond, total)
    total = add_image(own, others, total)

    image, near = measure_step(
        lists, valid, gathered, residual, cross, whitening, total, direction
    )
    mine = exchange(image, SAME_CORE)
    other = to_other_core(mine)
    solution_next, residual_next, scaled, back, old = spread_step(
        at, valid, into, self_at, mine, other, near, residual, solution, direction, cross, whitening
    )
    back = back[:PEERS] + to_other_core(back[PEERS:])
    direction_next = sum_step(exchange(back, SAME_CORE), scaled, direction, old)
    return (solution_next, residual_next, direction_next)


def solution(mesh):
    placed = (
        P(),
        P(),
        P(),
        P(("row", "col"), None, None, None),
        P(("row", "col"), None, None),
        P(("row", "col"), None, None),
        P(("row", "col"), None, None),
        P(("row", "col"), None, None),
    )
    return jax.shard_map(
        per_device,
        mesh=mesh,
        in_specs=placed,
        out_specs=(
            P(("row", "col"), None, None),
            P(("row", "col"), None, None),
            P(("row", "col"), None, None),
        ),
        check_vma=False,
    )
```

```python
import functools
import math

import jax
import jax.numpy as jnp
from jax import lax
from jax.experimental import pallas as pl
from jax.experimental.pallas import tpu as pltpu
from jax.sharding import PartitionSpec as P

f32 = jnp.float32
bf16 = jnp.bfloat16
rate = math.sqrt(3.0) / 0.3 * math.log2(math.e)
offset = 1.0 / math.log(2.0)
variance = -0.05 * math.e * math.log(2.0)
nugget = 1.0
AXES = ("row", "col")
BS, RHS, NBR, OWN = 256, 8, 4, 2
HALF = 128
PEERS = 64
GUARD = 2.0**-20
PAIR = 2 * OWN * BS
MEGA = 1 << 20


def split2(v):
    top = v.astype(bf16)
    return top, (v - top.astype(f32)).astype(bf16)


def split3(v):
    top = v.astype(bf16).astype(f32)
    rest = v - top
    middle = rest.astype(bf16).astype(f32)
    return top, middle, rest - middle


def pair_dot(a, top, low, dims):
    both = jnp.concatenate(split2(a), axis=0)
    high = lax.dot_general(both, top, (dims, ((), ())), preferred_element_type=f32)
    rest = lax.dot_general(both, low, (dims, ((), ())), preferred_element_type=f32)
    return high[:RHS] + (high[RHS:] + (rest[:RHS] + rest[RHS:]))


def features(place, own):
    a = (place - 0.5) * rate
    norm = jnp.sum(a * a, axis=0, keepdims=True)
    one = jnp.ones_like(norm)
    pad = jnp.zeros((3, norm.shape[1]), f32)
    parts = [-2.0 * a, one, norm, pad] if own else [a, norm, one, pad]
    top, middle, low = split3(jnp.concatenate(parts, axis=0))
    order = [top, middle, top, middle, low, top] if own else [top, top, middle, middle, top, low]
    return jnp.concatenate(order, axis=0).astype(bf16)


def places(tiles, block):
    rows = slice(3 * block, 3 * block + 3)
    return jnp.concatenate([tiles[4, rows, :], tiles[5, rows, :]], axis=1)


def pick_points(
    all_order, all_coordinates, direction_ref, out_ref, own_ref, order_ref, coordinates_ref, sems
):
    device = lax.axis_index("row") * 32 + lax.axis_index("col")
    pair = pl.multiple_of(device // 2 * PAIR, PAIR)
    order_copy = pltpu.make_async_copy(all_order.at[pl.ds(pair, PAIR)], order_ref, sems.at[0])
    order_copy.start()
    copy_points = pltpu.make_async_copy(all_coordinates, coordinates_ref, sems.at[1])
    copy_points.start()
    order_copy.wait()
    copy_points.wait()
    first = device % 2 * (OWN * BS)
    lane = lax.broadcasted_iota(jnp.int32, (3, HALF), 1)
    groups = 2 * OWN

    def one_point(i, found):
        kept = []
        for group in range(groups):
            at = order_ref[first + group * HALF + i]
            base = pl.multiple_of((at >> 7) << 7, HALF)
            line = coordinates_ref[:, pl.ds(base, HALF)]
            turned = pltpu.roll(line, (i - (at & (HALF - 1))) & (HALF - 1), 1)
            kept.append(jnp.where(lane == i, turned, found[group]))
        return tuple(kept)

    found = lax.fori_loop(0, HALF, one_point, (jnp.zeros((3, HALF), f32),) * groups, unroll=16)
    pad = jnp.zeros((2, HALF), f32)
    tiles = []
    for block in range(OWN):
        for half in range(2):
            tiles.append(direction_ref[block, :, half * HALF : (half + 1) * HALF])
    for half in range(2):
        tiles.append(jnp.concatenate([found[half], found[2 + half], pad], axis=0))

    for part, tile in enumerate(tiles):
        own_ref[part] = tile

    def copy(i, carry):
        for part, tile in enumerate(tiles):
            out_ref[i, part] = tile
        return carry

    lax.fori_loop(0, out_ref.shape[0], copy, 0)


def point_payload(ordering, coordinates, direction, copies):
    return pl.pallas_call(
        pick_points,
        out_shape=(
            jax.ShapeDtypeStruct((copies, 6, RHS, HALF), f32),
            jax.ShapeDtypeStruct((6, RHS, HALF), f32),
        ),
        in_specs=[
            pl.BlockSpec(memory_space=pltpu.HBM),
            pl.BlockSpec(memory_space=pltpu.HBM),
            pl.BlockSpec(memory_space=pltpu.VMEM),
        ],
        out_specs=(pl.BlockSpec(memory_space=pltpu.VMEM),) * 2,
        scratch_shapes=[
            pltpu.SMEM((PAIR,), jnp.int32),
            pltpu.VMEM(coordinates.shape, f32),
            pltpu.SemaphoreType.DMA((2,)),
        ],
        compiler_params=pltpu.CompilerParams(vmem_limit_bytes=56 * MEGA),
        name="pick_points",
    )(ordering, coordinates, direction)


TALL, WIDE = 512, 256


def image_kernel(pieces, own_ref, start_ref, *refs):
    columns, (out_ref, own_part, column_part, field_part, square) = refs[:pieces], refs[pieces:]
    each = pl.num_programs(0) // pieces
    step = columns[0].shape[0]

    @pl.when(pl.program_id(0) == 0)
    def _():
        for block in range(OWN):
            own_part[:, block * BS : (block + 1) * BS] = features(places(own_ref, block), True)
        out_ref[...] = start_ref[...]

    def prepare(columns_ref):
        for member in range(step):
            for block in range(OWN):
                at = OWN * member + block
                tiles = columns_ref.at[member]
                column_part[at * BS : (at + 1) * BS, :] = features(places(tiles, block), False).T
                field = jnp.concatenate([tiles[2 * block], tiles[2 * block + 1]], axis=1)
                field_part[at] = jnp.concatenate(split2(field * variance), axis=0)

    for index, columns_ref in enumerate(columns):
        pl.when(pl.program_id(0) // each == index)(functools.partial(prepare, columns_ref))
    jobs = [
        (q, r) for r in range(OWN * BS // WIDE) for q in range(step * OWN * BS // TALL)
    ]

    def fill(job, slot):
        q, r = jobs[job]
        square[slot] = jnp.dot(
            column_part[q * TALL : (q + 1) * TALL, :],
            own_part[:, r * WIDE : (r + 1) * WIDE],
            preferred_element_type=f32,
        )

    fill(0, 0)
    for job, (q, r) in enumerate(jobs):
        if job + 1 < len(jobs):
            fill(job + 1, (job + 1) % 2)
        for part in range(TALL // BS):
            for lanes in range(WIDE // HALF):
                x = square[
                    job % 2, part * BS : (part + 1) * BS, lanes * HALF : (lanes + 1) * HALF
                ]
                u = -offset - x * lax.rsqrt(jnp.maximum(x, GUARD))
                tile = u * jnp.exp2(u)
                top, low = split2(tile)
                field = field_part[q * (TALL // BS) + part]
                where = slice(r * WIDE + lanes * HALF, r * WIDE + (lanes + 1) * HALF)
                out_ref[:, where] += jnp.dot(
                    field, top, preferred_element_type=f32
                ) + jnp.dot(field, low, preferred_element_type=f32)


def add_image(own, columns, start, step):
    pieces, count = len(columns), columns[0].shape[0]
    each = count // step
    pairs = pieces * count * OWN * BS * OWN * BS

    def piece_spec(index):
        return pl.BlockSpec(
            (step, 6, RHS, HALF),
            lambda i: (jnp.clip(i - index * each, 0, each - 1), 0, 0, 0),
        )

    return pl.pallas_call(
        functools.partial(image_kernel, pieces),
        grid=(pieces * each,),
        in_specs=[
            pl.BlockSpec((6, RHS, HALF), lambda i: (0, 0, 0)),
            pl.BlockSpec((2 * RHS, OWN * BS), lambda i: (0, 0)),
        ]
        + [piece_spec(index) for index in range(pieces)],
        out_specs=pl.BlockSpec((2 * RHS, OWN * BS), lambda i: (0, 0)),
        out_shape=jax.ShapeDtypeStruct((2 * RHS, OWN * BS), f32),
        scratch_shapes=[
            pltpu.VMEM((48, OWN * BS), bf16),
            pltpu.VMEM((step * OWN * BS, 48), bf16),
            pltpu.VMEM((OWN * step, 2 * RHS, BS), bf16),
            pltpu.VMEM((2, TALL, WIDE), f32),
        ],
        compiler_params=pltpu.CompilerParams(vmem_limit_bytes=10 * MEGA),
        cost_estimate=pl.CostEstimate(
            flops=600 * pairs, transcendentals=2 * pairs, bytes_accessed=pieces * count * 6 * 4096
        ),
        name="image",
    )(own, start, *columns)


def split_whitening(whitening_ref, whiten_top, whiten_low):
    rows = lax.broadcasted_iota(jnp.int32, (BS, BS), 0)
    lanes = lax.broadcasted_iota(jnp.int32, (BS, BS), 1)
    for b in range(OWN):
        whiten = whitening_ref[b] + jnp.where(rows == lanes, 1.0, 0.0)
        whiten_top[b], whiten_low[b] = split2(whiten)


def fetch_factors(far_cross, far_whitening, cross_ref, whitening_ref, sems):
    copies = [
        pltpu.make_async_copy(far_cross.at[b], cross_ref.at[b], sems.at[b]) for b in range(OWN)
    ]
    copies.insert(OWN, pltpu.make_async_copy(far_whitening, whitening_ref, sems.at[OWN]))
    for copy in copies:
        copy.start()
    return copies


def lower(near, valid_ref, cross_ref, field, block):
    total = field
    for k in range(NBR):
        at = block * NBR + k
        weight = valid_ref[at].astype(f32)
        total = total - pair_dot(near(at) * weight, *split2(cross_ref[block, k]), ((1,), (1,)))
    return total


def lanes_of(v):
    return v[:, :HALF] + v[:, HALF:]


def measure_kernel(
    list_ref, valid_ref, all_ref, residual_ref, far_cross, far_whitening, sum_ref, direction_ref,
    out_ref, near_ref, near_buf, whiten_top, whiten_low, cross_ref, whitening_ref, sems,
    factor_sems,
):
    factors = fetch_factors(far_cross, far_whitening, cross_ref, whitening_ref, factor_sems)
    copies = []
    for b in range(OWN):
        for k in range(NBR):
            at = b * NBR + k
            copies.append(
                pltpu.make_async_copy(all_ref.at[list_ref[at]], near_buf.at[at], sems.at[at])
            )
            copies[-1].start()
    for copy in copies:
        copy.wait()
    factors[OWN].wait()
    split_whitening(whitening_ref, whiten_top, whiten_low)
    old = jnp.zeros((RHS, HALF), f32)
    curvature = jnp.zeros((RHS, HALF), f32)
    tiles = []
    for b in range(OWN):
        factors[b].wait()
        lowered = lower(
            lambda at: near_buf[at], valid_ref, cross_ref, residual_ref[b], b
        )
        mapped = pair_dot(lowered, whiten_top[b], whiten_low[b], ((1,), (1,)))
        old = old + lanes_of(mapped * mapped)
        here = slice(b * BS, (b + 1) * BS)
        image = sum_ref[:RHS, here] + sum_ref[RHS:, here] + nugget * direction_ref[b]
        curvature = curvature + lanes_of(direction_ref[b] * image)
        tiles += [image[:, :HALF], image[:, HALF:]]
    lane = lax.broadcasted_iota(jnp.int32, (RHS, HALF), 1)
    old = jnp.sum(old, axis=1, keepdims=True)
    curvature = jnp.sum(curvature, axis=1, keepdims=True)
    tiles.append(jnp.where(lane == 0, old, jnp.where(lane == 1, curvature, 0.0)))

    def copy(i, carry):
        for part, tile in enumerate(tiles):
            out_ref[i, part] = tile
        return carry

    lax.fori_loop(0, out_ref.shape[0], copy, 0)
    near_ref[...] = near_buf[...]


def measure_step(lists, valid, gathered, residual, cross, whitening, total, direction):
    smem = pl.BlockSpec(memory_space=pltpu.SMEM)
    vmem = pl.BlockSpec(memory_space=pltpu.VMEM)
    far = pl.BlockSpec(memory_space=pl.ANY)
    return pl.pallas_call(
        measure_kernel,
        out_shape=(
            jax.ShapeDtypeStruct((PEERS, 5, RHS, HALF), f32),
            jax.ShapeDtypeStruct((OWN * NBR, RHS, BS), f32),
        ),
        in_specs=[smem, smem, far, vmem, far, far, vmem, vmem],
        out_specs=(vmem, vmem),
        scratch_shapes=[
            pltpu.VMEM((OWN * NBR, RHS, BS), f32),
            pltpu.VMEM((OWN, BS, BS), bf16),
            pltpu.VMEM((OWN, BS, BS), bf16),
            pltpu.VMEM((OWN, NBR, BS, BS), f32),
            pltpu.VMEM((OWN, BS, BS), f32),
            pltpu.SemaphoreType.DMA((OWN * NBR,)),
            pltpu.SemaphoreType.DMA((OWN + 1,)),
        ],
        compiler_params=pltpu.CompilerParams(vmem_limit_bytes=12 * MEGA),
        name="measure_step",
    )(lists, valid, gathered, residual, cross, whitening, total, direction)


def spread_kernel(
    at_ref, valid_ref, into_ref, self_ref, mine_ref, other_ref, near_ref, residual_ref, solution_ref,
    direction_ref, far_cross, far_whitening,
    solution_out, residual_out, scaled_out, out_ref, old_out,
    whiten_top, whiten_low, cross_ref, whitening_ref, factor_sems,
):
    factors = fetch_factors(far_cross, far_whitening, cross_ref, whitening_ref, factor_sems)
    total = jnp.zeros((RHS, HALF), f32)
    for i in range(PEERS):
        total = total + mine_ref[i, 4] + other_ref[i, 4]
    old = total[:, 0:1]
    step = old / total[:, 1:2]

    def clear(i, carry):
        for part in range(2 * OWN):
            out_ref[i, part] = jnp.zeros((RHS, HALF), f32)
        return carry

    lax.fori_loop(0, 2 * PEERS, clear, 0)

    def image_of(at):
        slot = at & 63
        a = jnp.concatenate([mine_ref[slot, 2 * (at >> 7)], mine_ref[slot, 2 * (at >> 7) + 1]], 1)
        b = jnp.concatenate([other_ref[slot, 2 * (at >> 7)], other_ref[slot, 2 * (at >> 7) + 1]], 1)
        return jnp.where(((at >> 6) & 1) == 0, a, b)

    newer = jnp.zeros((RHS, HALF), f32)
    factors[OWN].wait()
    split_whitening(whitening_ref, whiten_top, whiten_low)
    for b in range(OWN):
        factors[b].wait()
        solution_out[b] = solution_ref[b] + step * direction_ref[b]
        image = jnp.concatenate(
            [mine_ref[self_ref[0], 2 * b], mine_ref[self_ref[0], 2 * b + 1]], 1
        )
        following = residual_ref[b] - step * image
        residual_out[b] = following
        lowered = lower(
            lambda at: near_ref[at] - step * image_of(at_ref[at]),
            valid_ref, cross_ref, following, b,
        )
        mapped = pair_dot(lowered, whiten_top[b], whiten_low[b], ((1,), (1,)))
        newer = newer + lanes_of(mapped * mapped)
        scaled = pair_dot(mapped, whiten_top[b], whiten_low[b], ((1,), (0,)))
        scaled_out[b] = scaled
        for k in range(NBR):
            at = b * NBR + k
            spread = pair_dot(scaled, *split2(cross_ref[b, k]), ((1,), (0,)))
            spread = spread * valid_ref[at].astype(f32)
            to = into_ref[at]
            out_ref[to >> 1, 2 * (to & 1)] += spread[:, :HALF]
            out_ref[to >> 1, 2 * (to & 1) + 1] += spread[:, HALF:]
    newer = jnp.sum(newer, axis=1, keepdims=True)
    lane = lax.broadcasted_iota(jnp.int32, (RHS, HALF), 1)
    newer = jnp.where(lane == 0, newer, 0.0)

    def share(i, carry):
        out_ref[i, 2 * OWN] = newer
        return carry

    lax.fori_loop(0, 2 * PEERS, share, 0)
    old_out[...] = jnp.broadcast_to(old, (RHS, HALF))


def sum_kernel(all_ref, scaled_ref, direction_ref, old_ref, out_ref):
    total = all_ref[0]
    for i in range(1, PEERS):
        total = total + all_ref[i]
    ratio = total[2 * OWN, :, 0:1] / old_ref[:, 0:1]
    for b in range(OWN):
        back = jnp.concatenate([total[2 * b], total[2 * b + 1]], axis=1)
        out_ref[b] = scaled_ref[b] - back + ratio * direction_ref[b]


def sum_step(everything, scaled, direction, old):
    vmem = pl.BlockSpec(memory_space=pltpu.VMEM)
    return pl.pallas_call(
        sum_kernel,
        out_shape=jax.ShapeDtypeStruct((OWN, RHS, BS), f32),
        in_specs=[vmem] * 4,
        out_specs=vmem,
        compiler_params=pltpu.CompilerParams(vmem_limit_bytes=8 * MEGA),
        name="sum_step",
    )(everything, scaled, direction, old)


def spread_step(
    at, valid, into, self_at, mine, other, near, residual, solution, direction, cross, whitening
):
    smem = pl.BlockSpec(memory_space=pltpu.SMEM)
    vmem = pl.BlockSpec(memory_space=pltpu.VMEM)
    own = jax.ShapeDtypeStruct((OWN, RHS, BS), f32)
    return pl.pallas_call(
        spread_kernel,
        out_shape=(
            own,
            own,
            own,
            jax.ShapeDtypeStruct((2 * PEERS, 2 * OWN + 1, RHS, HALF), f32),
            jax.ShapeDtypeStruct((RHS, HALF), f32),
        ),
        in_specs=[smem] * 4 + [vmem] * 6 + [pl.BlockSpec(memory_space=pl.ANY)] * 2,
        out_specs=(vmem,) * 5,
        scratch_shapes=[
            pltpu.VMEM((OWN, BS, BS), bf16),
            pltpu.VMEM((OWN, BS, BS), bf16),
            pltpu.VMEM((OWN, NBR, BS, BS), f32),
            pltpu.VMEM((OWN, BS, BS), f32),
            pltpu.SemaphoreType.DMA((OWN + 1,)),
        ],
        compiler_params=pltpu.CompilerParams(vmem_limit_bytes=20 * MEGA),
        name="spread_step",
    )(
        at, valid, into, self_at, mine, other, near, residual, solution, direction, cross, whitening
    )


def x_around(hop):
    def target(i):
        return (i // 8 + hop) % 4 * 8 + i % 8

    return functools.partial(
        lax.ppermute, axis_name="col", perm=[(i, target(i)) for i in range(32)]
    )


def to_other_core(value):
    return lax.ppermute(value, "col", [(i, i ^ 1) for i in range(32)])


def exchange(value, groups):
    return lax.all_to_all(value, AXES, 0, 0, axis_index_groups=groups, tiled=True)


SAME_CORE = [[2 * j + core for j in range(PEERS)] for core in range(2)]
SAME_X_CORE = [
    [y * 32 + x * 8 + z * 2 + core for y in range(4) for z in range(4)]
    for x in range(4)
    for core in range(2)
]


def per_device(coordinates, ordering, neighbours, cross, whitening, solution, residual, direction):
    row = lax.axis_index("row")
    col = lax.axis_index("col")
    device = row * 32 + col
    here_core = device % 2
    own_ids = device * OWN + jnp.arange(OWN, dtype=jnp.int32)
    own_lists = lax.dynamic_slice_in_dim(neighbours, device * OWN, OWN, 0)
    valid = (own_lists < own_ids[:, None]).astype(jnp.int32).reshape(-1)
    lists = own_lists.reshape(-1)
    their = lists // OWN
    core_gap = (their % 2) ^ here_core
    at = ((lists % OWN) * 2 + core_gap) * PEERS + their // 2
    into = (core_gap * PEERS + their // 2) * OWN + lists % OWN
    self_at = (device // 2)[None]

    gathered = lax.all_gather(residual, AXES, axis=0, tiled=True)

    payload, own = point_payload(ordering, coordinates, direction, 16)
    plane = exchange(payload, SAME_X_CORE)
    plane, plane_other = lax.optimization_barrier((plane, to_other_core(plane)))
    beyond = [x_around(hop)(plane) for hop in (1, 3, 2)]
    total = add_image(own, [plane, plane_other], jnp.zeros((2 * RHS, OWN * BS), f32), 8)
    others = [to_other_core(piece) for piece in beyond]
    total = add_image(own, beyond, total, 16)
    total = add_image(own, others, total, 16)

    image, near = measure_step(
        lists, valid, gathered, residual, cross, whitening, total, direction
    )
    mine = exchange(image, SAME_CORE)
    other = to_other_core(mine)
    solution_next, residual_next, scaled, back, old = spread_step(
        at, valid, into, self_at, mine, other, near, residual, solution, direction, cross, whitening
    )
    back = back[:PEERS] + to_other_core(back[PEERS:])
    direction_next = sum_step(exchange(back, SAME_CORE), scaled, direction, old)
    return (solution_next, residual_next, direction_next)


def solution(mesh):
    placed = (
        P(),
        P(),
        P(),
        P(("row", "col"), None, None, None),
        P(("row", "col"), None, None),
        P(("row", "col"), None, None),
        P(("row", "col"), None, None),
        P(("row", "col"), None, None),
    )
    return jax.shard_map(
        per_device,
        mesh=mesh,
        in_specs=placed,
        out_specs=(
            P(("row", "col"), None, None),
            P(("row", "col"), None, None),
            P(("row", "col"), None, None),
        ),
        check_vma=False,
    )
```
